256 devices in a mesh: dp: 4 (over x), expert: 16 (over z, core), tp: 4 (over y).
Axes of the slice: x: 4, y: 4, z: 8, core: 2. Of those that a mesh axis runs over, the one named last changes fastest.
Arguments:
- hidden: bfloat16 [16, 64, 96, 5632], P('expert', 'dp', None, 'tp'), parts along dimension 1, may hold values from -6 to 6
- down_weight: bfloat16 [16, 5632, 3072], P('expert', 'tp'), may hold values from -0.078125 to 0.078125
- routes: int32 [16384, 4], P(('dp', 'expert')), parts along dimension 0, may hold values from 0 to 15, all different within a row; in each aligned block of 256 rows (0 to 255, 256 to 511, ...) at most 96 rows name the same one
- route_weight: float32 [16384, 4], P(('dp', 'expert')), parts along dimension 0, may hold values from 0.05 to 1
- residual: bfloat16 [16384, 3072], P(('dp', 'expert'), 'tp'), parts along dimension 0, may hold values from -6 to 6
Outputs:
- mixed: bfloat16 [16384, 3072], P(('dp', 'expert'), 'tp'), parts along dimension 0
The draws below stay inside these ranges and needn't reach their ends.
There are 4 independent parts, one for each index of `dp`. The reference program is written for one: setup_inputs(seed, part) draws one part's arguments, and reference() takes and returns one part's arrays. A program takes and returns all parts, laid end to end along the dimension named above; an argument that names none is the same for every part. Nothing has to cross between parts.
Inputs may be any that keep to these rules, and one draw needn't show every extreme that they name: `routes`: each row names 4 different experts. Among the 256 rows of one source group no expert is named by more than 96 rows, a bound that some of them reach.
All inputs are finite; a program needn't handle non-finite values.
Results may differ from the reference program's by a relative error of at most 0.0095.
Values may be sent and summed in bfloat16 or wider, within the bound.
A program may use at most 128 MiB of HBM per device.

```python
import math
import jax
import jax.numpy as jnp
import numpy as np
from jax import lax

D = 3072
FF = 5632
EXPERTS = 16
TOP = 4
TOK_DEV = 256
CAP = 96
SOURCES = 16
GROUPS = 4
HID_DEV = 1408
TOKENS = 4096


def shard_levels(stream_key, shape, split, smallest, high):
    level, own = 1.0, jax.random.fold_in(stream_key, 6)
    for dim, shards_of in split:
        heights = jnp.exp(jax.random.uniform(jax.random.fold_in(own, dim), (shards_of,), jnp.float32, smallest / len(split), high / len(split)))
        level = level * jnp.repeat(heights, shape[dim] // shards_of).reshape([-1 if axis == dim else 1 for axis in range(len(shape))])
    return level


def deal_out(stream_key, own, number, rows, amount, top, limit, lean):
    ranking = jax.random.permutation(stream_key, amount)
    crowded, ordinary = shares(amount, rows * top, limit, lean, True), shares(amount, rows * top, limit, lean, False)
    places = jnp.arange(amount)

    def named(tallies, turn):
        used = int((tallies > 0).sum())
        fixed = max(1, used // 4)
        moved = fixed + (places - fixed + turn * (used - fixed)) % max(1, amount - fixed)
        return jnp.zeros((amount,), jnp.int32).at[ranking[jnp.where(places < fixed, places, moved)]].set(jnp.asarray(tallies, jnp.int32))

    tallies = jnp.where(number % 4 == 0, named(crowded, number // 4), named(ordinary, number - number // 4 - 1))
    mixed = jax.random.permutation(jax.random.fold_in(own, 3), amount)
    giver, taker = mixed[0:amount // 2 * 2:2], mixed[1:amount // 2 * 2:2]
    slack = jnp.minimum(tallies[giver] - 1, limit - tallies[taker]) // 2
    slack = jnp.where((giver == ranking[0]) | (taker == ranking[0]) | (tallies[taker] == 0), 0, jnp.maximum(slack, 0))
    moved = jax.random.randint(jax.random.fold_in(own, 4), (amount // 2,), 0, 1 << 20) % (slack + 1)
    tallies = tallies.at[giver].add(-moved).at[taker].add(moved)
    members = jnp.searchsorted(jnp.cumsum(tallies), jnp.arange(rows * top), side="right").astype(jnp.int32)
    table = members.reshape(top, rows).T
    table = table[jax.random.permutation(jax.random.fold_in(own, 1), rows)]
    turn = jax.random.randint(jax.random.fold_in(own, 2), (rows, 1), 0, top)
    return jnp.take_along_axis(table, (jnp.arange(top)[None, :] + turn) % top, axis=1)


def shares(count, total, bound, lean, full):
    weights = [(1 << 20) // math.isqrt(standing ** lean) + 1 for standing in range(1, count + 1)]
    largest = bound if full else min(bound, max(-(-total // count), total * weights[0] // sum(weights)))
    least = 1 if total - largest >= count - 1 else 0
    counts, surplus = [largest] + [least] * (count - 1), total - largest - least * (count - 1)
    while surplus > 0:
        free = [i for i in range(1, count) if counts[i] < largest] or [i for i in range(1, count) if counts[i] < bound]
        mass, budget = sum([weights[i] for i in free]), surplus
        for i in free:
            extra = min(bound - counts[i], max(1, budget * weights[i] // mass), surplus)
            counts[i] = counts[i] + extra
            surplus = surplus - extra
    return np.array(counts)


def scatter_about(key, shape, width, limit, split=(), held_as=jnp.bfloat16):
    entries = jax.random.normal(key, shape, jnp.float32) * width
    if len(split) > 0:
        entries = shard_levels(key, shape, split, -0.22, 0.18) * entries
    return jnp.clip(entries, min=-limit, max=limit).astype(held_as)


def setup_inputs(seed: int = 0, part: int = 0) -> dict:
    key_list = jax.random.split(jax.random.key(seed), 6)
    own_keys = jax.random.split(jax.random.fold_in(key_list[5], part), 6)
    hidden = scatter_about(own_keys[0], (EXPERTS, SOURCES, CAP, FF), 1.0, 6.0, ((0, 16), (3, 4)))
    down_weight = scatter_about(key_list[1], (EXPERTS, FF, D), FF ** -0.5, 0.078125, ((0, 16), (1, 4)))
    routes_keys = jax.random.split(jax.random.fold_in(own_keys[2], 1), TOKENS // TOK_DEV)
    routes_turns = jax.random.permutation(jax.random.fold_in(own_keys[2], 3), TOKENS // TOK_DEV)
    routes = jax.vmap(lambda own, number: deal_out(jax.random.fold_in(own_keys[2], 2), own, number, TOK_DEV, EXPERTS, TOP, CAP, 2))(routes_keys, routes_turns).reshape((TOKENS, TOP))
    route_weight = jnp.clip(jnp.exp(math.log(1.0) - 2.9957323 * jax.random.uniform(own_keys[3], (TOKENS, TOP), jnp.float32) ** shard_levels(own_keys[3], (TOKENS, TOP), ((0, 16),), -0.2, 0.2)), 0.05, 1.0)
    residual = scatter_about(own_keys[4], (TOKENS, D), 1.0, 6.0, ((0, 16), (1, 4)))
    return {"hidden": hidden, "down_weight": down_weight, "routes": routes, "route_weight": route_weight, "residual": residual}


def one_expert(operands):
    block_hidden, block_weight = operands
    hidden_groups = block_hidden.reshape(SOURCES * CAP, GROUPS, HID_DEV)
    weight_groups = block_weight.reshape(GROUPS, HID_DEV, D)
    running = jnp.zeros((SOURCES * CAP, D), jnp.float32)
    for group in range(GROUPS):
        partial_value = jnp.dot(hidden_groups[:, group, :], weight_groups[group], preferred_element_type=jnp.float32).astype(jnp.bfloat16)
        partial_value = lax.optimization_barrier(partial_value)
        running = running + partial_value.astype(jnp.float32)
    return running.reshape(SOURCES, CAP, D)


def reference(hidden, down_weight, routes, route_weight, residual):
    expert_out = lax.map(one_expert, (hidden, down_weight))
    grouped = routes.reshape(SOURCES, TOK_DEV, TOP)
    expert_ids = jnp.arange(EXPERTS, dtype=jnp.int32)
    onehot = jnp.sum((grouped[:, :, :, None] == expert_ids[None, None, None, :]).astype(jnp.int32), axis=2)
    before = jnp.cumsum(onehot, axis=1) - onehot
    slot_of = jnp.take_along_axis(before, grouped, axis=2).astype(jnp.int32)
    source_index = jnp.arange(SOURCES, dtype=jnp.int32)[:, None, None]
    picked = expert_out[grouped, source_index, slot_of]
    weights = route_weight.reshape(SOURCES, TOK_DEV, TOP)
    share = weights / jnp.sum(weights, axis=2, keepdims=True)
    expert_mix = jnp.sum(share[:, :, :, None] * picked, axis=2).reshape(TOKENS, D)
    return (residual.astype(jnp.float32) + expert_mix).astype(jnp.bfloat16)
```

```python
import functools

import jax
import jax.numpy as jnp
from jax import lax
from jax.experimental import pallas as pl
from jax.experimental.pallas import tpu as pltpu
from jax.sharding import PartitionSpec as P

MESH = pl.DeviceIdType.MESH

ORDER = (
    (4, 0), (4, 1), (3, 0), (-3, 0), (3, 1), (-3, 1), (2, 0), (-2, 0),
    (2, 1), (-2, 1), (1, 0), (-1, 0), (1, 1), (-1, 1), (0, 0), (0, 1),
)
PAIRS = len(ORDER) // 2
SLICE_SHIFT = (3, 1, 2, 0)
HOPS = ((0, 2, 1, 3), (1, 2, 0, 3))
COLUMN_TILE = 256


def kernel(
    hidden, weight, routes, route_weight, residual, out,
    w_buf, h_buf, part, ring_in, mixed_in, pick_hi, pick_lo,
    w_sem, h_sem, ring_send, ring_recv, z_send, z_recv,
):
    expert, tp = lax.axis_index("expert"), lax.axis_index("tp")
    n_tp = len(SLICE_SHIFT)
    cap, width = part.shape[2], part.shape[3]
    tokens, top = routes.shape
    chips = len(ORDER) // 2
    z, core = expert // 2, expert % 2
    up, down = lax.rem(tp + 1, n_tp), lax.rem(tp + n_tp - 1, n_tp)

    def place(shift, other):
        chip = lax.rem(z + (shift + chips), chips)
        return 2 * chip + (core if other == 0 else 1 - core)

    targets = [place(shift, other) for shift, other in ORDER]
    senders = [place(-shift, other) for shift, other in ORDER]

    barrier = pltpu.get_barrier_semaphore()
    for peer in (up, down):
        pl.semaphore_signal(barrier, inc=1, device_id={"tp": peer}, device_id_type=MESH)
    for k, (shift, other) in enumerate(ORDER):
        if (shift, other) != (0, 0):
            pl.semaphore_signal(barrier, inc=1, device_id={"expert": targets[k]}, device_id_type=MESH)

    def w_load(r):
        start = pl.multiple_of(lax.rem(tp + SLICE_SHIFT[r], n_tp) * width, width)
        return pltpu.make_async_copy(weight.at[0, :, pl.ds(start, width)], w_buf.at[r], w_sem.at[r])

    def h_load(k):
        return pltpu.make_async_copy(hidden.at[0, targets[k]], h_buf.at[k], h_sem.at[k])

    h_load(0).start()
    h_load(1).start()
    for r in range(n_tp):
        w_load(r).start()
    for k in range(2, len(ORDER)):
        h_load(k).start()

    lane = lax.broadcasted_iota(jnp.int32, (8, len(ORDER)), 1)
    ids = jnp.zeros((8, len(ORDER)), jnp.int32)
    for k in range(len(ORDER)):
        ids = jnp.where(lane == k, senders[k], ids)
    ids = jnp.broadcast_to(ids[0:1, :], (tokens, len(ORDER)))
    scores = route_weight[...]
    share = scores / jnp.sum(scores, axis=1, keepdims=True)
    chosen = routes[...]
    member = jnp.zeros((tokens, len(ORDER)), jnp.float32)
    portion = jnp.zeros((tokens, len(ORDER)), jnp.float32)
    for c in range(top):
        same = chosen[:, c : c + 1] == ids
        member = member + jnp.where(same, 1.0, 0.0)
        portion = portion + jnp.where(same, share[:, c : c + 1], 0.0)
    rows = lax.broadcasted_iota(jnp.int32, (tokens, tokens), 0)
    cols = lax.broadcasted_iota(jnp.int32, (tokens, tokens), 1)
    earlier = jnp.where(cols < rows, 1.0, 0.0).astype(jnp.bfloat16)
    before = jnp.dot(earlier, member.astype(jnp.bfloat16), preferred_element_type=jnp.float32)
    slot = jnp.where(member > 0.5, before.astype(jnp.int32), -len(ORDER) * cap)
    portion_hi = portion.astype(jnp.bfloat16).astype(jnp.float32)
    portion_lo = portion - portion_hi
    groups = pick_hi.shape[0]
    per_group = len(ORDER) // groups
    column = lax.broadcasted_iota(jnp.int32, (tokens, per_group * cap), 1)
    for g in range(groups):
        hi = jnp.zeros((tokens, per_group * cap), jnp.float32)
        lo = jnp.zeros((tokens, per_group * cap), jnp.float32)
        for q in range(per_group):
            k = g * per_group + q
            hit = column == slot[:, k : k + 1] + q * cap
            hi = jnp.where(hit, portion_hi[:, k : k + 1], hi)
            lo = jnp.where(hit, portion_lo[:, k : k + 1], lo)
        pick_hi[g] = hi.astype(jnp.bfloat16)
        pick_lo[g] = lo.astype(jnp.bfloat16)

    def ring_copy(i, way, hop):
        k = 2 * i + way
        return pltpu.make_async_remote_copy(
            src_ref=part.at[k, HOPS[way][hop]],
            dst_ref=ring_in.at[hop, k],
            send_sem=ring_send.at[hop, k],
            recv_sem=ring_recv.at[hop, k],
            device_id={"tp": (up, down)[way]},
            device_id_type=MESH,
        )

    def z_copy(k, target):
        return pltpu.make_async_remote_copy(
            src_ref=part.at[k, n_tp - 1],
            dst_ref=mixed_in.at[k],
            send_sem=z_send.at[k],
            recv_sem=z_recv.at[k],
            device_id={"expert": target},
            device_id_type=MESH,
        )

    def matmul(i, r):
        left = h_buf[pl.ds(2 * i, 2)].reshape(2 * cap, h_buf.shape[2])

        def tile(t, carry):
            at = pl.ds(pl.multiple_of(t * COLUMN_TILE, COLUMN_TILE), COLUMN_TILE)
            product = jnp.dot(left, w_buf[r, :, at], preferred_element_type=jnp.float32)
            part[pl.ds(2 * i, 2), r, :, at] = product.astype(jnp.bfloat16).reshape(2, cap, COLUMN_TILE)
            return carry

        lax.fori_loop(0, width // COLUMN_TILE, tile, 0)

    def arrive(i, hop):
        for way in range(2):
            ring_copy(i, way, hop).wait_recv()
        for way in range(2):
            k, r = 2 * i + way, HOPS[way][hop + 1]
            part[k, r] = part[k, r] + ring_in[hop, k]

    def step(n, carry):
        @pl.when(n < PAIRS)
        def _():
            for way in range(2):
                h = 2 * n + way
                pltpu.make_async_copy(hidden.at[0, 0], h_buf.at[h], h_sem.at[h]).wait()
            for r in range(n_tp):
                @pl.when(n == 0)
                def _():
                    w_load(r).wait()
                matmul(n, r)
                if r == 1:
                    @pl.when(n == 0)
                    def _():
                        pl.semaphore_wait(barrier, len(ORDER) + 1)
                    ring_copy(n, 0, 0).start()
                if r == 2:
                    ring_copy(n, 1, 0).start()

        for hop in range(2):
            i = n - 1 - hop

            @pl.when((i >= 0) & (i < PAIRS))
            def _():
                arrive(i, hop)
                for way in range(2):
                    ring_copy(i, way, hop + 1).start()

        i = n - 3

        @pl.when((i >= 0) & (i < PAIRS - 1))
        def _():
            arrive(i, 2)
            for way in range(2):
                shift = jnp.where(i == 0, 4, 3 - (i - 1) // 2)
                other = jnp.where(i == 0, way, lax.rem(i - 1, 2))
                chip = lax.rem(z + chips + (shift if way == 0 else -shift), chips)
                place_core = jnp.where(other == 0, core, 1 - core)
                z_copy(2 * i + way, 2 * chip + place_core).start()

        return carry

    lax.fori_loop(0, PAIRS + 2, step, 0)

    own, partner = len(ORDER) - 2, len(ORDER) - 1
    arrive(PAIRS - 1, 2)
    z_copy(partner, targets[partner]).start()
    mixed_in[own] = part[own, n_tp - 1]

    def taken(g):
        block = mixed_in[g * per_group : (g + 1) * per_group].reshape(per_group * cap, width)
        return jnp.dot(pick_hi[g], block, preferred_element_type=jnp.float32) + jnp.dot(
            pick_lo[g], block, preferred_element_type=jnp.float32
        )

    total = residual[...].astype(jnp.float32)
    for g in range(groups):
        for k in range(g * per_group, (g + 1) * per_group):
            if k != own:
                z_copy(k, targets[k]).wait_recv()
        total = total + taken(g)
    out[...] = total.astype(jnp.bfloat16)

    def drain(k, carry):
        for hop in range(3):
            pltpu.make_async_remote_copy(
                src_ref=part.at[k, 0], dst_ref=ring_in.at[hop, k],
                send_sem=ring_send.at[hop, k], recv_sem=ring_recv.at[hop, k],
                device_id={"tp": up}, device_id_type=MESH,
            ).wait_send()
        return carry

    lax.fori_loop(0, len(ORDER), drain, 0)
    for k in range(len(ORDER)):
        if k != own:
            z_copy(k, targets[k]).wait_send()


def on_device(hidden, down_weight, routes, route_weight, residual):
    sources, cap, units = hidden.shape[1:]
    tokens, width = residual.shape
    n_tp = len(SLICE_SHIFT)
    bf16 = jnp.bfloat16
    any_space = pl.BlockSpec(memory_space=pl.ANY)
    vmem = pl.BlockSpec(memory_space=pltpu.VMEM)
    groups = 4
    return pl.pallas_call(
        kernel,
        out_shape=jax.ShapeDtypeStruct((tokens, width), bf16),
        in_specs=[any_space, any_space, vmem, vmem, vmem],
        out_specs=vmem,
        scratch_shapes=[
            pltpu.VMEM((n_tp, units, width), bf16),
            pltpu.VMEM((sources, cap, units), bf16),
            pltpu.VMEM((sources, n_tp, cap, width), bf16),
            pltpu.VMEM((n_tp - 1, sources, cap, width), bf16),
            pltpu.VMEM((sources, cap, width), bf16),
            pltpu.VMEM((groups, tokens, sources // groups * cap), bf16),
            pltpu.VMEM((groups, tokens, sources // groups * cap), bf16),
            pltpu.SemaphoreType.DMA((n_tp,)),
            pltpu.SemaphoreType.DMA((sources,)),
            pltpu.SemaphoreType.DMA((n_tp - 1, sources)),
            pltpu.SemaphoreType.DMA((n_tp - 1, sources)),
            pltpu.SemaphoreType.DMA((sources,)),
            pltpu.SemaphoreType.DMA((sources,)),
        ],
        compiler_params=pltpu.CompilerParams(
            collective_id=0, has_side_effects=True, vmem_limit_bytes=60 * 1024 * 1024
        ),
        name="moe_down_combine",
    )(hidden, down_weight, routes, route_weight, residual)


def solution(mesh):
    return jax.shard_map(
        on_device,
        mesh=mesh,
        in_specs=(
            P("expert", "dp", None, "tp"),
            P("expert", "tp", None),
            P(("dp", "expert"), None),
            P(("dp", "expert"), None),
            P(("dp", "expert"), "tp"),
        ),
        out_specs=P(("dp", "expert"), "tp"),
        check_vma=False,
    )
```

```python
import jax
import jax.numpy as jnp
from jax import lax
from jax.experimental import pallas as pl
from jax.experimental.pallas import tpu as pltpu
from jax.sharding import PartitionSpec as P

MESH = pl.DeviceIdType.MESH

CHIPS = 8
LAST = CHIPS - 1
SLICE_SHIFT = (3, 1, 2, 0)
HOPS = ((0, 2, 1, 3), (1, 2, 0, 3))
TP_FIRST = 512
STREAM = 256


def kernel(
    hidden, weight, routes, scores, residual, out,
    w_buf, h_buf, part, ring_in, blocks, hand_b, hand_a, tok, tok_in, late, late_in,
    all_routes, all_scores, counts, table, pick_hi, pick_lo,
    w_sem, h_sem, ring_send, ring_recv, hb_send, hb_recv, ha_send, ha_recv, tok_send, tok_recv,
    late_send, late_recv, route_send, route_recv, score_send, score_recv,
):
    expert, tp = lax.axis_index("expert"), lax.axis_index("tp")
    n_tp = len(SLICE_SHIFT)
    cap, width = part.shape[2], residual.shape[1]
    tokens = residual.shape[0]
    half = tokens // 2
    f32, bf16 = jnp.float32, jnp.bfloat16
    z, core = expert // 2, lax.rem(expert, 2)
    up, down = lax.rem(tp + 1, n_tp), lax.rem(tp + n_tp - 1, n_tp)
    partner = 2 * z + 1 - core

    def chip(shift):
        return lax.rem(z + shift + CHIPS, CHIPS)

    def ahead(i):
        return (CHIPS // 2 - (i + 1) // 2) * (1 if i % 2 == 1 else -1)

    barrier = pltpu.get_barrier_semaphore()
    for peer in (up, down):
        pl.semaphore_signal(barrier, inc=1, device_id={"tp": peer}, device_id_type=MESH)
    pl.semaphore_signal(barrier, inc=1, device_id={"expert": partner}, device_id_type=MESH)
    for i in range(LAST):
        peer = 2 * chip(-ahead(i)) + core
        pl.semaphore_signal(barrier, inc=1, device_id={"expert": peer}, device_id_type=MESH)

    def w_load(r):
        start = pl.multiple_of(lax.rem(tp + SLICE_SHIFT[r], n_tp) * width, width)
        return pltpu.make_async_copy(weight.at[0, :, pl.ds(start, width)], w_buf.at[r], w_sem.at[r])

    def h_load(i, other):
        source = 2 * chip(ahead(i)) + (1 - core if other else core)
        return pltpu.make_async_copy(hidden.at[0, source], h_buf.at[2 * i + other], h_sem.at[2 * i + other])

    for other in range(2):
        h_load(0, other).start()
    for r in range(n_tp):
        w_load(r).start()
    for i in range(1, CHIPS):
        for other in range(2):
            h_load(i, other).start()

    def route_copies(i):
        peer = {"expert": 2 * chip(-ahead(i)) + core}
        return [
            pltpu.make_async_remote_copy(
                src_ref=src, dst_ref=dst.at[i], send_sem=send.at[i], recv_sem=recv.at[i],
                device_id=peer, device_id_type=MESH,
            )
            for src, dst, send, recv in (
                (routes, all_routes, route_send, route_recv),
                (scores, all_scores, score_send, score_recv),
            )
        ]

    def ring_copy(i, way, hop):
        k = 2 * i + way
        return pltpu.make_async_remote_copy(
            src_ref=part.at[k, HOPS[way][hop]],
            dst_ref=ring_in.at[hop, k],
            send_sem=ring_send.at[hop, k],
            recv_sem=ring_recv.at[hop, k],
            device_id={"tp": (up, down)[way]},
            device_id_type=MESH,
        )

    def late_copy(way, hop):
        return pltpu.make_async_remote_copy(
            src_ref=late.at[HOPS[way][hop], pl.ds(way * half, half)],
            dst_ref=late_in.at[hop, way],
            send_sem=late_send.at[hop, way],
            recv_sem=late_recv.at[hop, way],
            device_id={"tp": (up, down)[way]},
            device_id_type=MESH,
        )

    def hand_copy(i, early):
        first, count = (n_tp, TP_FIRST // STREAM) if early else (0, n_tp)
        source, send, recv = (hand_a, ha_send, ha_recv) if early else (hand_b, hb_send, hb_recv)
        return pltpu.make_async_remote_copy(
            src_ref=source.at[i],
            dst_ref=blocks.at[i, pl.ds(first, count), 1],
            send_sem=send.at[i],
            recv_sem=recv.at[i],
            device_id={"expert": partner},
            device_id_type=MESH,
        )

    def tok_copy(i, s, target):
        return pltpu.make_async_remote_copy(
            src_ref=tok.at[i, s],
            dst_ref=tok_in.at[i, s],
            send_sem=tok_send.at[i, s],
            recv_sem=tok_recv.at[i, s],
            device_id={"expert": 2 * target + core},
            device_id_type=MESH,
        )

    def left_rows(i):
        return h_buf[pl.ds(2 * i, 2)].reshape(2 * cap, h_buf.shape[2])

    def await_rows(i):
        for other in range(2):
            k = 2 * i + other
            pltpu.make_async_copy(hidden.at[0, 0], h_buf.at[k], h_sem.at[k]).wait()

    def matmul_early(i, first):
        left = left_rows(i)
        for r in range(n_tp):
            if first:
                w_load(r).wait()

            def tile(t, carry):
                at = pl.ds(pl.multiple_of(t * STREAM, STREAM), STREAM)
                product = jnp.dot(left, w_buf[r, :, at], preferred_element_type=f32)
                part[pl.ds(2 * i, 2), r, :, at] = product.astype(bf16).reshape(2, cap, STREAM)
                return carry

            lax.fori_loop(0, TP_FIRST // STREAM, tile, 0)
            if r == 1:
                if first:
                    pl.semaphore_wait(barrier, LAST + 3)
                ring_copy(i, 0, 0).start()
            if r == 2:
                ring_copy(i, 1, 0).start()

    def matmul_late(i, carry):
        left = left_rows(i)

        def tile(r, inner):
            product = jnp.dot(left, w_buf[r, :, TP_FIRST:], preferred_element_type=f32).astype(bf16)
            blocks[i, r, 0] = product[:cap]
            hand_b[i, r] = product[cap:]
            return inner

        lax.fori_loop(0, n_tp, tile, 0)
        hand_copy(i, False).start()
        return carry

    def arrive(i, hop):
        for way in range(2):
            ring_copy(i, way, hop).wait_recv()
        for way in range(2):
            k, r = 2 * i + way, HOPS[way][hop + 1]
            value = part[k, r] + ring_in[hop, k]
            if hop < n_tp - 2:
                part[k, r] = value
            else:
                for h in range(TP_FIRST // STREAM):
                    piece = value[:, h * STREAM : (h + 1) * STREAM]
                    if way == 0:
                        blocks[i, n_tp + h, 0] = piece
                    else:
                        hand_a[i, h] = piece

    def weighted(i, s):
        rows = blocks[i, s].reshape(2 * cap, STREAM)
        return jnp.dot(pick_hi[i], rows, preferred_element_type=f32) + jnp.dot(
            pick_lo[i], rows, preferred_element_type=f32
        )

    def chain(i, first, count, early):
        hand_copy(i, early).wait_recv()

        def one(s, carry):
            forward = (s < 2) | (s == n_tp)
            total = weighted(i, s)
            begins = (i == 0) | (i == jnp.where(forward, 2, 1))

            @pl.when(begins)
            def _():
                tok[i, s] = total.astype(bf16)

            @pl.when(jnp.logical_not(begins))
            def _():
                source = jnp.maximum(i - 2, 0)
                tok_copy(source, s, z).wait_recv()
                tok[i, s] = (total + tok_in[source, s].astype(f32)).astype(bf16)

            onward = jnp.where(i == 0, forward, lax.rem(i, 2) == 1)
            tok_copy(i, s, chip(jnp.where(onward, 1, -1))).start()
            return carry

        lax.fori_loop(first, first + count, one, 0)

    def chain_end(s):
        for i in (LAST - 2, LAST - 1):
            tok_copy(i, s, z).wait_recv()
        return weighted(LAST, s) + tok_in[LAST - 2, s].astype(f32) + tok_in[LAST - 1, s].astype(f32)

    def chain_late(i, carry):
        chain(i, 0, n_tp, False)
        return carry

    def chain_early(i, carry):
        chain(i, n_tp, TP_FIRST // STREAM, True)
        return carry

    await_rows(0)
    matmul_early(0, True)
    for i in range(LAST):
        for copy in route_copies(i):
            copy.start()
    all_routes[LAST] = routes[...]
    all_scores[LAST] = scores[...]
    matmul_late(0, 0)
    await_rows(1)
    matmul_early(1, False)
    await_rows(2)

    rows = lax.broadcasted_iota(jnp.int32, (tokens, tokens), 0)
    cols = lax.broadcasted_iota(jnp.int32, (tokens, tokens), 1)
    earlier = jnp.where(rows < cols, 1.0, 0.0).astype(bf16)
    for i in range(CHIPS):
        if i < LAST:
            for copy in route_copies(i):
                copy.wait_recv()
        chosen, value = all_routes[i], all_scores[i]
        share = value / jnp.sum(value, axis=0, keepdims=True)
        for q, e in enumerate((expert, partner)):
            same = chosen == e
            line = pl.ds(2 * i + q, 1)
            counts[line, :] = jnp.sum(jnp.where(same, 1.0, 0.0), axis=0, keepdims=True)
            table[pl.ds(4 * CHIPS + 2 * i + q, 1), :] = jnp.sum(jnp.where(same, share, 0.0), axis=0, keepdims=True)
    member = counts[...]
    before = jnp.dot(member.astype(bf16), earlier, preferred_element_type=f32)
    second = lax.rem(lax.broadcasted_iota(jnp.int32, member.shape, 0), 2) == 1
    portion = table[4 * CHIPS : 6 * CHIPS, :]
    portion_hi = portion.astype(bf16).astype(f32)
    table[0 : 2 * CHIPS, :] = jnp.where(member > 0.5, before + jnp.where(second, float(cap), 0.0), -1.0)
    table[2 * CHIPS : 4 * CHIPS, :] = portion_hi
    table[4 * CHIPS : 6 * CHIPS, :] = portion - portion_hi
    table[6 * CHIPS :, :] = jnp.zeros((table.shape[0] - 6 * CHIPS, tokens), f32)
    upright = jnp.transpose(table[...])
    column = lax.broadcasted_iota(jnp.int32, (tokens, 2 * cap), 1).astype(f32)
    for i in range(CHIPS):
        own, other = (
            column == upright[:, 2 * i + q : 2 * i + q + 1] for q in range(2)
        )
        for pick, base in ((pick_hi, 2 * CHIPS), (pick_lo, 4 * CHIPS)):
            a, b = (upright[:, base + 2 * i + q : base + 2 * i + q + 1] for q in range(2))
            pick[i] = jnp.where(own, a, jnp.where(other, b, 0.0)).astype(bf16)

    chain_late(0, 0)

    def step(n, carry):
        @pl.when(n + 2 < CHIPS)
        def _():
            await_rows(n + 2)

        @pl.when(n + 1 < CHIPS)
        def _():
            matmul_early(n + 1, False)

        for hop in range(n_tp - 1):
            i = n - 1 - hop

            @pl.when((i >= 0) & (i < CHIPS))
            def _():
                arrive(i, hop)
                if hop < n_tp - 2:
                    for way in range(2):
                        ring_copy(i, way, hop + 1).start()
                else:
                    hand_copy(i, True).start()

        odd = lax.rem(n, 2) == 1
        begin = jnp.where(n == 1, 1, jnp.where(odd, CHIPS, n + 1))
        end = jnp.where(n == 1, 3, jnp.minimum(n + 3, CHIPS))
        lax.fori_loop(begin, end, matmul_late, 0)
        lax.fori_loop(jnp.where(odd, n, LAST), jnp.minimum(n + 2, LAST), chain_late, 0)
        lax.fori_loop(jnp.where(odd, jnp.maximum(n - 4, 0), LAST), jnp.minimum(n - 2, LAST), chain_early, 0)

        @pl.when(n == LAST)
        def _():
            hand_copy(LAST, False).wait_recv()
            for s in range(n_tp):
                late[s] = chain_end(s).astype(bf16)
            for way in range(2):
                late_copy(way, 0).start()

        for hop in range(n_tp - 2):
            @pl.when(n == CHIPS + hop)
            def _():
                for way in range(2):
                    late_copy(way, hop).wait_recv()
                for way in range(2):
                    here = pl.ds(way * half, half)
                    r = HOPS[way][hop + 1]
                    late[r, here] = late[r, here] + late_in[hop, way]
                for way in range(2):
                    late_copy(way, hop + 1).start()

        return carry

    lax.fori_loop(1, CHIPS + n_tp - 1, step, 0)

    for way in range(2):
        late_copy(way, n_tp - 2).wait_recv()
        here = slice(way * half, (way + 1) * half)
        mixed = late[n_tp - 1, here].astype(f32) + late_in[n_tp - 2, way].astype(f32)
        out[here, TP_FIRST:] = (residual[here, TP_FIRST:].astype(f32) + mixed).astype(bf16)
    hand_copy(LAST, True).wait_recv()
    for h in range(TP_FIRST // STREAM):
        at = slice(h * STREAM, (h + 1) * STREAM)
        out[:, at] = (residual[:, at].astype(f32) + chain_end(n_tp + h)).astype(bf16)

    def drain(i, carry):
        for hop in range(n_tp - 1):
            for way in range(2):
                ring_copy(i, way, hop).wait_send()
        for early in (False, True):
            hand_copy(i, early).wait_send()

        @pl.when(i < LAST)
        def _():
            for s in range(blocks.shape[1]):
                tok_copy(i, s, z).wait_send()

        return carry

    lax.fori_loop(0, CHIPS, drain, 0)
    for i in range(LAST):
        for copy in route_copies(i):
            copy.wait_send()
    for hop in range(n_tp - 1):
        for way in range(2):
            late_copy(way, hop).wait_send()


def on_device(hidden, down_weight, routes, route_weight, residual):
    sources, cap, units = hidden.shape[1:]
    tokens, width = residual.shape
    top = routes.shape[1]
    n_tp = len(SLICE_SHIFT)
    early = TP_FIRST // STREAM
    streams = n_tp + early
    bf16, f32 = jnp.bfloat16, jnp.float32
    any_space = pl.BlockSpec(memory_space=pl.ANY)
    vmem = pl.BlockSpec(memory_space=pltpu.VMEM)
    dma = pltpu.SemaphoreType.DMA
    return pl.pallas_call(
        kernel,
        out_shape=jax.ShapeDtypeStruct((tokens, width), bf16),
        in_specs=[any_space, any_space, vmem, vmem, vmem],
        out_specs=vmem,
        scratch_shapes=[
            pltpu.VMEM((n_tp, units, width), bf16),
            pltpu.VMEM((sources, cap, units), bf16),
            pltpu.VMEM((sources, n_tp, cap, TP_FIRST), bf16),
            pltpu.VMEM((n_tp - 1, sources, cap, TP_FIRST), bf16),
            pltpu.VMEM((CHIPS, streams, 2, cap, STREAM), bf16),
            pltpu.VMEM((CHIPS, n_tp, cap, STREAM), bf16),
            pltpu.VMEM((CHIPS, early, cap, STREAM), bf16),
            pltpu.VMEM((LAST, streams, tokens, STREAM), bf16),
            pltpu.VMEM((LAST, streams, tokens, STREAM), bf16),
            pltpu.VMEM((n_tp, tokens, STREAM), bf16),
            pltpu.VMEM((n_tp - 1, 2, tokens // 2, STREAM), bf16),
            pltpu.VMEM((CHIPS, top, tokens), jnp.int32),
            pltpu.VMEM((CHIPS, top, tokens), f32),
            pltpu.VMEM((2 * CHIPS, tokens), f32),
            pltpu.VMEM((128, tokens), f32),
            pltpu.VMEM((CHIPS, tokens, 2 * cap), bf16),
            pltpu.VMEM((CHIPS, tokens, 2 * cap), bf16),
            dma((n_tp,)),
            dma((sources,)),
            dma((n_tp - 1, sources)),
            dma((n_tp - 1, sources)),
            dma((CHIPS,)),
            dma((CHIPS,)),
            dma((CHIPS,)),
            dma((CHIPS,)),
            dma((LAST, streams)),
            dma((LAST, streams)),
            dma((n_tp - 1, 2)),
            dma((n_tp - 1, 2)),
            dma((LAST,)),
            dma((LAST,)),
            dma((LAST,)),
            dma((LAST,)),
        ],
        compiler_params=pltpu.CompilerParams(
            collective_id=0, has_side_effects=True, vmem_limit_bytes=60 * 1024 * 1024
        ),
        name="moe_down_combine",
    )(hidden, down_weight, routes.T, route_weight.T, residual)


def solution(mesh):
    return jax.shard_map(
        on_device,
        mesh=mesh,
        in_specs=(
            P("expert", "dp", None, "tp"),
            P("expert", "tp", None),
            P(("dp", "expert"), None),
            P(("dp", "expert"), None),
            P(("dp", "expert"), "tp"),
        ),
        out_specs=P(("dp", "expert"), "tp"),
        check_vma=False,
    )
```

```python
import jax
import jax.numpy as jnp
from jax import lax
from jax.experimental import pallas as pl
from jax.experimental.pallas import tpu as pltpu
from jax.sharding import PartitionSpec as P

MESH = pl.DeviceIdType.MESH

CHIPS = 8
LAST = CHIPS - 1
SLICE_SHIFT = (3, 1, 2, 0)
HOPS = ((0, 2, 1, 3), (1, 2, 0, 3))
TP_FIRST = 512
STREAM = 256

ORDER = (
    64, 1, 2, 3, 8, 72, 9, 10, 11, 16, 80, 128, 384, 520, 528, 201, 209, 202,
    210, 203, 136, 211, 17, 18, 19, 24, 88, 25, 26, 27, 32, 96, 536, 33, 34, 144,
    217, 35, 544, 225, 137, 129, 40, 104, 152, 218, 226, 41, 42, 160, 43, 48, 112, 219,
    227, 145, 49, 50, 51, 56, 120, 552, 560, 57, 58, 59, 458, 450, 233, 241, 525, 153,
    234, 242, 168, 161, 235, 243, 466, 264, 532, 176, 204, 213, 184, 257, 474, 169, 541, 482,
    258, 177, 259, 320, 548, 185, 490, 220, 229, 498, 557, 321, 564, 506, 236, 245, 322,
)


WORDS = tuple(
    sum(code << 10 * j for j, code in enumerate(ORDER[t : t + 3])) for t in range(0, len(ORDER), 3)
)


def kernel(
    hidden, weight, routes, scores, residual, out,
    w_early, w_late, h_buf, part, ring_in, blocks, hand_b, hand_a, raw_in, tok, tok_in, late, late_in,
    all_routes, all_scores, counts, table, pick_hi, pick_lo,
    we_sem, wl_sem, h_sem, ring_send, ring_recv, hb_send, hb_recv, ha_send, ha_recv, raw_send, raw_recv,
    tok_send, tok_recv, late_send, late_recv, route_send, route_recv, score_send, score_recv,
):
    expert, tp = lax.axis_index("expert"), lax.axis_index("tp")
    n_tp = len(SLICE_SHIFT)
    n_early = TP_FIRST // STREAM
    cap, width = part.shape[2], residual.shape[1]
    tokens = residual.shape[0]
    half = tokens // 2
    f32, bf16 = jnp.float32, jnp.bfloat16
    z, core = expert // 2, lax.rem(expert, 2)
    up, down = lax.rem(tp + 1, n_tp), lax.rem(tp + n_tp - 1, n_tp)
    partner = 2 * z + 1 - core

    def chip(shift):
        return lax.rem(z + shift + CHIPS, CHIPS)

    def ahead(i):
        return (CHIPS // 2 - (i + 1) // 2) * (1 if i % 2 == 1 else -1)

    barrier = pltpu.get_barrier_semaphore()
    for peer in (up, down):
        pl.semaphore_signal(barrier, inc=1, device_id={"tp": peer}, device_id_type=MESH)
    greeted = [2 * chip(-ahead(i)) + core for i in range(1, LAST)]
    greeted += [partner, 2 * chip(1) + 1 - core, 2 * chip(-1) + 1 - core]
    for peer in greeted:
        pl.semaphore_signal(barrier, inc=1, device_id={"expert": peer}, device_id_type=MESH)

    def w_load(r, early):
        start = lax.rem(tp + SLICE_SHIFT[r], n_tp) * width
        if early:
            at = pl.ds(pl.multiple_of(start, STREAM), TP_FIRST)
            return pltpu.make_async_copy(weight.at[0, :, at], w_early.at[r], we_sem.at[r])
        at = pl.ds(pl.multiple_of(start + TP_FIRST, STREAM), STREAM)
        return pltpu.make_async_copy(
            weight.at[0, :, at], w_late.at[:, pl.ds(r * STREAM, STREAM)], wl_sem.at[r]
        )

    def h_load(i, other):
        source = 2 * chip(ahead(i)) + (1 - core if other else core)
        return pltpu.make_async_copy(hidden.at[0, source], h_buf.at[2 * i + other], h_sem.at[2 * i + other])

    for other in range(2):
        h_load(0, other).start()
    w_load(0, True).start()
    for r in range(n_tp):
        w_load(r, False).start()
    for r in range(1, n_tp):
        w_load(r, True).start()
    for i in range(1, CHIPS):
        for other in range(2):
            h_load(i, other).start()

    def route_copies(i):
        peer = {"expert": 2 * chip(-ahead(i)) + core}
        return [
            pltpu.make_async_remote_copy(
                src_ref=src, dst_ref=dst.at[i], send_sem=send.at[i], recv_sem=recv.at[i],
                device_id=peer, device_id_type=MESH,
            )
            for src, dst, send, recv in (
                (routes, all_routes, route_send, route_recv),
                (scores, all_scores, score_send, score_recv),
            )
        ]

    def ring_part(way, hop):
        first, second = HOPS[way][0], HOPS[way][2]
        return jnp.where(hop == 0, first, jnp.where(hop == 2, second, 2))

    def ring_copy(i, way, hop):
        k = 2 * i + way
        return pltpu.make_async_remote_copy(
            src_ref=part.at[k, ring_part(way, hop)],
            dst_ref=ring_in.at[hop, k],
            send_sem=ring_send.at[hop, k],
            recv_sem=ring_recv.at[hop, k],
            device_id={"tp": (up, down)[way]},
            device_id_type=MESH,
        )

    def late_copy(way, hop):
        return pltpu.make_async_remote_copy(
            src_ref=late.at[ring_part(way, hop), pl.ds(way * half, half)],
            dst_ref=late_in.at[hop, way],
            send_sem=late_send.at[hop, way],
            recv_sem=late_recv.at[hop, way],
            device_id={"tp": (up, down)[way]},
            device_id_type=MESH,
        )

    def hand_copy(i, early):
        first, count = (n_tp, n_early) if early else (0, n_tp)
        source, send, recv = (hand_a, ha_send, ha_recv) if early else (hand_b, hb_send, hb_recv)
        return pltpu.make_async_remote_copy(
            src_ref=source.at[i],
            dst_ref=blocks.at[i, pl.ds(first, count), 1],
            send_sem=send.at[i],
            recv_sem=recv.at[i],
            device_id={"expert": partner},
            device_id_type=MESH,
        )

    def goes_up(s):
        return s in (0, 1, n_tp)

    def raw_copy(s, other):
        source = (hand_b.at[0, s] if s < n_tp else hand_a.at[0, s - n_tp]) if other else blocks.at[0, s, 0]
        return pltpu.make_async_remote_copy(
            src_ref=source,
            dst_ref=raw_in.at[s, other],
            send_sem=raw_send.at[s, other],
            recv_sem=raw_recv.at[s, other],
            device_id={"expert": 2 * chip(1 if goes_up(s) else -1) + (1 - core if other else core)},
            device_id_type=MESH,
        )

    def raw_wait(s):
        for other in range(2):
            pltpu.make_async_remote_copy(
                src_ref=raw_in.at[s, other], dst_ref=raw_in.at[s, other],
                send_sem=raw_send.at[s, other], recv_sem=raw_recv.at[s, other],
                device_id={"expert": partner}, device_id_type=MESH,
            ).wait_recv()

    def tok_copy(i, s, target):
        return pltpu.make_async_remote_copy(
            src_ref=tok.at[i - 1, s],
            dst_ref=tok_in.at[i - 1, s],
            send_sem=tok_send.at[i - 1, s],
            recv_sem=tok_recv.at[i - 1, s],
            device_id={"expert": 2 * target + core},
            device_id_type=MESH,
        )

    def left_rows(i):
        return h_buf[pl.ds(2 * i, 2)].reshape(2 * cap, h_buf.shape[2])

    def await_rows(i):
        for other in range(2):
            k = 2 * i + other
            pltpu.make_async_copy(hidden.at[0, 0], h_buf.at[k], h_sem.at[k]).wait()

    def product_early(i, r):
        product = jnp.dot(left_rows(i), w_early[r], preferred_element_type=f32)
        part[pl.ds(2 * i, 2), r] = product.astype(bf16).reshape(2, cap, TP_FIRST)

    def matmul_early(i, r):
        for way in range(n_tp - 1):
            @pl.when((i == 0) & (r == way + 1))
            def _():
                w_load(way + 1, True).wait()

        @pl.when(r == 0)
        def _():
            await_rows(i)

        product_early(i, r)
        for way in range(2):
            @pl.when(r == way)
            def _():
                ring_copy(i, way, 0).start()

    def matmul_late(i, x):
        @pl.when(i == 0)
        def _():
            for r in range(n_tp):
                w_load(r, False).wait()

        product = jnp.dot(left_rows(i), w_late[...], preferred_element_type=f32).astype(bf16)
        for r in range(n_tp):
            piece = product[:, r * STREAM : (r + 1) * STREAM]
            blocks[i, r, 0] = piece[:cap]
            hand_b[i, r] = piece[cap:]

        @pl.when(i == 0)
        def _():
            for s in range(n_tp):
                for other in range(2):
                    raw_copy(s, other).start()

        @pl.when(i > 0)
        def _():
            hand_copy(i, False).start()

    def arrive(i, hop):
        for way in range(2):
            ring_copy(i, way, hop).wait_recv()
        for way in range(2):
            k, r = 2 * i + way, ring_part(way, hop + 1)
            part[k, r] = part[k, r] + ring_in[hop, k]
        for way in range(2):
            ring_copy(i, way, hop + 1).start()

    def arrive_last(i, x):
        hop = n_tp - 2
        for way in range(2):
            ring_copy(i, way, hop).wait_recv()
        for way in range(2):
            k = 2 * i + way
            for h in range(n_early):
                at = slice(h * STREAM, (h + 1) * STREAM)
                piece = part[k, n_tp - 1, :, at] + ring_in[hop, k, :, at]
                if way == 0:
                    blocks[i, n_tp + h, 0] = piece
                else:
                    hand_a[i, h] = piece

        @pl.when(i == 0)
        def _():
            for s in range(n_tp, n_tp + n_early):
                for other in range(2):
                    raw_copy(s, other).start()

        @pl.when(i > 0)
        def _():
            hand_copy(i, True).start()

    def pick(j, rows):
        return jnp.dot(pick_hi[j], rows, preferred_element_type=f32) + jnp.dot(
            pick_lo[j], rows, preferred_element_type=f32
        )

    def weighted(i, s):
        return pick(i, blocks[i, s].reshape(2 * cap, STREAM))

    def chain(i, s):
        total = weighted(i, s)
        forward = (s < 2) | (s == n_tp)

        @pl.when(i > 2)
        def _():
            tok_copy(i - 2, s, z).wait_recv()
            tok[i - 1, s] = (total + tok_in[i - 3, s].astype(f32)).astype(bf16)

        raw = i == jnp.where(forward, 1, 2)

        @pl.when(raw)
        def _():
            raw_wait(s)
            more = pick(jnp.where(forward, 0, CHIPS), raw_in[s].reshape(2 * cap, STREAM))
            tok[i - 1, s] = (total + more).astype(bf16)

        @pl.when((i < 3) & jnp.logical_not(raw))
        def _():
            tok[i - 1, s] = total.astype(bf16)

        tok_copy(i, s, chip(jnp.where(lax.rem(i, 2) == 1, 1, -1))).start()

    def chain_first(i, s):
        @pl.when(s < n_tp)
        def _():
            hand_copy(i, False).wait_recv()

        @pl.when(s >= n_tp)
        def _():
            hand_copy(i, True).wait_recv()

        chain(i, s)

    def chain_end(s):
        for i in (LAST - 2, LAST - 1):
            tok_copy(i, s, z).wait_recv()
        return weighted(LAST, s) + tok_in[LAST - 3, s].astype(f32) + tok_in[LAST - 2, s].astype(f32)

    def end_late(first, s):
        @pl.when(first == 1)
        def _():
            hand_copy(LAST, False).wait_recv()

        late[s] = chain_end(s).astype(bf16)

    def late_step(i, x):
        @pl.when(x > 0)
        def _():
            for way in range(2):
                late_copy(way, x - 1).wait_recv()
            for way in range(2):
                here = pl.ds(way * half, half)
                r = ring_part(way, x)
                late[r, here] = late[r, here] + late_in[x - 1, way]

        for way in range(2):
            late_copy(way, x).start()

    def selection(i, x):
        rows = lax.broadcasted_iota(jnp.int32, (tokens, tokens), 0)
        cols = lax.broadcasted_iota(jnp.int32, (tokens, tokens), 1)
        earlier = jnp.where(rows < cols, 1.0, 0.0).astype(bf16)
        sets = CHIPS + 1
        for j in range(1, LAST):
            for copy in route_copies(j):
                copy.wait_recv()
        for j in range(sets):
            group, shift = ((1, -1) if j == 0 else (2, 1) if j == CHIPS else (j, 0))
            chosen, value = all_routes[group], all_scores[group]
            share = value / jnp.sum(value, axis=0, keepdims=True)
            for q in range(2):
                same = chosen == 2 * chip(shift) + (1 - core if q else core)
                line = 2 * j + q
                counts[line : line + 1, :] = jnp.sum(jnp.where(same, 1.0, 0.0), axis=0, keepdims=True)
                table[96 + line : 97 + line, :] = jnp.sum(jnp.where(same, share, 0.0), axis=0, keepdims=True)
        counts[2 * sets :, :] = jnp.zeros((counts.shape[0] - 2 * sets, tokens), f32)
        table[96 + 2 * sets :, :] = jnp.zeros((32 - 2 * sets, tokens), f32)
        member = counts[...]
        before = jnp.dot(member.astype(bf16), earlier, preferred_element_type=f32)
        second = lax.rem(lax.broadcasted_iota(jnp.int32, member.shape, 0), 2) == 1
        portion = table[96:128, :]
        portion_hi = portion.astype(bf16).astype(f32)
        table[0:32, :] = jnp.where(member > 0.5, before + jnp.where(second, float(cap), 0.0), -1.0)
        table[32:64, :] = portion_hi
        table[64:96, :] = portion - portion_hi
        upright = jnp.transpose(table[...])
        column = lax.broadcasted_iota(jnp.int32, (tokens, 2 * cap), 1).astype(f32)
        for j in range(sets):
            own, other = (column == upright[:, 2 * j + q : 2 * j + q + 1] for q in range(2))
            for target, base in ((pick_hi, 32), (pick_lo, 64)):
                a, b = (upright[:, base + 2 * j + q : base + 2 * j + q + 1] for q in range(2))
                target[j] = jnp.where(own, a, jnp.where(other, b, 0.0)).astype(bf16)

    kinds = (
        matmul_early, matmul_late, arrive, chain, end_late, late_step, selection, arrive_last, chain_first,
    )

    w_load(0, True).wait()
    await_rows(0)
    product_early(0, 0)
    pl.semaphore_wait(barrier, 2 + len(greeted))
    for i in range(1, LAST):
        for copy in route_copies(i):
            copy.start()
    ring_copy(0, 0, 0).start()
    all_routes[LAST] = routes[...]
    all_scores[LAST] = scores[...]

    def step(t, carry):
        word = jnp.int32(WORDS[0])
        for j in range(1, len(WORDS)):
            word = jnp.where(t >= 3 * j, WORDS[j], word)
        code = lax.rem(lax.shift_right_logical(word, 10 * lax.rem(t, 3)), 1024)
        i, x = lax.rem(code // 8, 8), lax.rem(code, 8)

        def branch(kind):
            def run():
                kind(i, x)

            return run

        lax.switch(code // 64, [branch(kind) for kind in kinds])
        return carry

    lax.fori_loop(0, len(ORDER), step, 0)

    for way in range(2):
        late_copy(way, n_tp - 2).wait_recv()
        here = slice(way * half, (way + 1) * half)
        mixed = late[n_tp - 1, here].astype(f32) + late_in[n_tp - 2, way].astype(f32)
        out[here, TP_FIRST:] = (residual[here, TP_FIRST:].astype(f32) + mixed).astype(bf16)
    hand_copy(LAST, True).wait_recv()
    for h in range(n_early):
        at = slice(h * STREAM, (h + 1) * STREAM)
        out[:, at] = (residual[:, at].astype(f32) + chain_end(n_tp + h)).astype(bf16)

    def drain(i, carry):
        for hop in range(n_tp - 1):
            for way in range(2):
                ring_copy(i, way, hop).wait_send()

        @pl.when(i > 0)
        def _():
            for early in (False, True):
                hand_copy(i, early).wait_send()

        @pl.when((i > 0) & (i < LAST))
        def _():
            for s in range(blocks.shape[1]):
                tok_copy(i, s, z).wait_send()

        return carry

    lax.fori_loop(0, CHIPS, drain, 0)
    for s in range(blocks.shape[1]):
        for other in range(2):
            raw_copy(s, other).wait_send()
    for i in range(1, LAST):
        for copy in route_copies(i):
            copy.wait_send()
    for hop in range(n_tp - 1):
        for way in range(2):
            late_copy(way, hop).wait_send()


def on_device(hidden, down_weight, routes, route_weight, residual):
    sources, cap, units = hidden.shape[1:]
    tokens, width = residual.shape
    top = routes.shape[1]
    n_tp = len(SLICE_SHIFT)
    early = TP_FIRST // STREAM
    streams = n_tp + early
    bf16, f32 = jnp.bfloat16, jnp.float32
    any_space = pl.BlockSpec(memory_space=pl.ANY)
    vmem = pl.BlockSpec(memory_space=pltpu.VMEM)
    dma = pltpu.SemaphoreType.DMA
    return pl.pallas_call(
        kernel,
        out_shape=jax.ShapeDtypeStruct((tokens, width), bf16),
        in_specs=[any_space, any_space, vmem, vmem, vmem],
        out_specs=vmem,
        scratch_shapes=[
            pltpu.VMEM((n_tp, units, TP_FIRST), bf16),
            pltpu.VMEM((units, n_tp * STREAM), bf16),
            pltpu.VMEM((sources, cap, units), bf16),
            pltpu.VMEM((sources, n_tp, cap, TP_FIRST), bf16),
            pltpu.VMEM((n_tp - 1, sources, cap, TP_FIRST), bf16),
            pltpu.VMEM((CHIPS, streams, 2, cap, STREAM), bf16),
            pltpu.VMEM((CHIPS, n_tp, cap, STREAM), bf16),
            pltpu.VMEM((CHIPS, early, cap, STREAM), bf16),
            pltpu.VMEM((streams, 2, cap, STREAM), bf16),
            pltpu.VMEM((LAST - 1, streams, tokens, STREAM), bf16),
            pltpu.VMEM((LAST - 1, streams, tokens, STREAM), bf16),
            pltpu.VMEM((n_tp, tokens, STREAM), bf16),
            pltpu.VMEM((n_tp - 1, 2, tokens // 2, STREAM), bf16),
            pltpu.VMEM((CHIPS, top, tokens), jnp.int32),
            pltpu.VMEM((CHIPS, top, tokens), f32),
            pltpu.VMEM((32, tokens), f32),
            pltpu.VMEM((128, tokens), f32),
            pltpu.VMEM((CHIPS + 1, tokens, 2 * cap), bf16),
            pltpu.VMEM((CHIPS + 1, tokens, 2 * cap), bf16),
            dma((n_tp,)),
            dma((n_tp,)),
            dma((sources,)),
            dma((n_tp - 1, sources)),
            dma((n_tp - 1, sources)),
            dma((CHIPS,)),
            dma((CHIPS,)),
            dma((CHIPS,)),
            dma((CHIPS,)),
            dma((streams, 2)),
            dma((streams, 2)),
            dma((LAST - 1, streams)),
            dma((LAST - 1, streams)),
            dma((n_tp - 1, 2)),
            dma((n_tp - 1, 2)),
            dma((LAST,)),
            dma((LAST,)),
            dma((LAST,)),
            dma((LAST,)),
        ],
        compiler_params=pltpu.CompilerParams(
            collective_id=0, has_side_effects=True, vmem_limit_bytes=60 * 1024 * 1024
        ),
        name="moe_down_combine",
    )(hidden, down_weight, routes.T, route_weight.T, residual)


def solution(mesh):
    return jax.shard_map(
        on_device,
        mesh=mesh,
        in_specs=(
            P("expert", "dp", None, "tp"),
            P("expert", "tp", None),
            P(("dp", "expert"), None),
            P(("dp", "expert"), None),
            P(("dp", "expert"), "tp"),
        ),
        out_specs=P(("dp", "expert"), "tp"),
        check_vma=False,
    )
```

```python
import jax
import jax.numpy as jnp
from jax import lax
from jax.experimental import pallas as pl
from jax.experimental.pallas import tpu as pltpu
from jax.sharding import PartitionSpec as P

MESH = pl.DeviceIdType.MESH

CHIPS = 8
LAST = CHIPS - 1
SLICE_SHIFT = (3, 1, 2, 0)
HOPS = ((0, 2, 1, 3), (1, 2, 0, 3))
TP_FIRST = 512
STREAM = 256

SETS = ((1, -1), (1, 0), (2, 0), (3, 0), (4, 0), (5, 0), (6, 0), (7, 0), (2, 1), (3, -1), (4, 1))

ORDER = (
    1, 2, 3, 8, 9, 16, 17, 18, 19, 10, 11, 128, 72, 80, 136, 384, 385, 144,
    521, 531, 210, 386, 200, 129, 24, 88, 32, 137, 96, 33, 538, 145, 219, 217, 544, 227,
    225, 34, 387, 25, 40, 226, 104, 41, 42, 43, 160, 26, 554, 27, 458, 450, 216, 235,
    35, 48, 49, 50, 152, 51, 233, 466, 112, 168, 56, 120, 57, 560, 243, 242, 161, 241,
    58, 59, 176, 533, 524, 153, 169, 232, 184, 267, 482, 548, 177, 258, 474, 257, 540, 221,
    490, 256, 320, 229, 185, 498, 556, 321, 564, 237, 245, 506, 322, 576, 576,
)
WORDS = tuple(
    sum(code << 10 * j for j, code in enumerate(ORDER[t : t + 3])) for t in range(0, len(ORDER), 3)
)


def kernel(
    hidden, weight, routes, scores, residual, out,
    w_early, w_late, h_buf, part, ring_in, blocks, hand_b, hand_a, raw_in, tok, tok_in, late, late_in,
    all_routes, all_scores, counts, table, upright, pick_hi, pick_lo,
    we_sem, wl_sem, h_sem, ring_send, ring_recv, hb_send, hb_recv, ha_send, ha_recv, raw_send, raw_recv,
    tok_send, tok_recv, late_send, late_recv, route_send, route_recv, score_send, score_recv,
):
    expert, tp = lax.axis_index("expert"), lax.axis_index("tp")
    n_tp = len(SLICE_SHIFT)
    n_early = TP_FIRST // STREAM
    cap, width = part.shape[2], residual.shape[1]
    tokens = residual.shape[0]
    half = tokens // 2
    f32, bf16 = jnp.float32, jnp.bfloat16
    z, core = expert // 2, lax.rem(expert, 2)
    up, down = lax.rem(tp + 1, n_tp), lax.rem(tp + n_tp - 1, n_tp)
    partner = 2 * z + 1 - core

    def chip(shift):
        return lax.rem(z + shift + CHIPS, CHIPS)

    def ahead(i):
        return (CHIPS // 2 - (i + 1) // 2) * (1 if i % 2 == 1 else -1)

    barrier = pltpu.get_barrier_semaphore()
    for peer in (up, down):
        pl.semaphore_signal(barrier, inc=1, device_id={"tp": peer}, device_id_type=MESH)
    greeted = [2 * chip(-ahead(i)) + core for i in range(1, LAST)]
    greeted += [partner, 2 * chip(1) + 1 - core, 2 * chip(-1) + 1 - core]
    for peer in greeted:
        pl.semaphore_signal(barrier, inc=1, device_id={"expert": peer}, device_id_type=MESH)

    def w_load(r, early):
        start = lax.rem(tp + SLICE_SHIFT[r], n_tp) * width
        if early:
            at = pl.ds(pl.multiple_of(start, STREAM), TP_FIRST)
            return pltpu.make_async_copy(weight.at[0, :, at], w_early.at[r], we_sem.at[r])
        at = pl.ds(pl.multiple_of(start + TP_FIRST, STREAM), STREAM)
        return pltpu.make_async_copy(
            weight.at[0, :, at], w_late.at[:, pl.ds(r * STREAM, STREAM)], wl_sem.at[r]
        )

    def h_load(i, other):
        source = 2 * chip(ahead(i)) + (1 - core if other else core)
        return pltpu.make_async_copy(hidden.at[0, source], h_buf.at[2 * i + other], h_sem.at[2 * i + other])

    for other in range(2):
        h_load(0, other).start()
    for r in range(n_tp):
        w_load(r, False).start()
    for r in range(n_tp):
        w_load(r, True).start()
    for i in range(1, CHIPS):
        for other in range(2):
            h_load(i, other).start()

    def route_copies(i):
        peer = {"expert": 2 * chip(-ahead(i)) + core}
        return [
            pltpu.make_async_remote_copy(
                src_ref=src, dst_ref=dst.at[i], send_sem=send.at[i], recv_sem=recv.at[i],
                device_id=peer, device_id_type=MESH,
            )
            for src, dst, send, recv in (
                (routes, all_routes, route_send, route_recv),
                (scores, all_scores, score_send, score_recv),
            )
        ]

    def ring_part(way, hop):
        first, second = HOPS[way][0], HOPS[way][2]
        return jnp.where(hop == 0, first, jnp.where(hop == 2, second, 2))

    def ring_copy(i, way, hop):
        k = 2 * i + way
        return pltpu.make_async_remote_copy(
            src_ref=part.at[k, ring_part(way, hop)],
            dst_ref=ring_in.at[hop, k],
            send_sem=ring_send.at[hop, k],
            recv_sem=ring_recv.at[hop, k],
            device_id={"tp": (up, down)[way]},
            device_id_type=MESH,
        )

    def late_copy(way, hop):
        return pltpu.make_async_remote_copy(
            src_ref=late.at[ring_part(way, hop), pl.ds(way * half, half)],
            dst_ref=late_in.at[hop, way],
            send_sem=late_send.at[hop, way],
            recv_sem=late_recv.at[hop, way],
            device_id={"tp": (up, down)[way]},
            device_id_type=MESH,
        )

    def hand_copy(i, early):
        first, count = (n_tp, n_early) if early else (0, n_tp)
        source, send, recv = (hand_a, ha_send, ha_recv) if early else (hand_b, hb_send, hb_recv)
        return pltpu.make_async_remote_copy(
            src_ref=source.at[i],
            dst_ref=blocks.at[i, pl.ds(first, count), 1],
            send_sem=send.at[i],
            recv_sem=recv.at[i],
            device_id={"expert": partner},
            device_id_type=MESH,
        )

    def goes_up(s):
        return s in (0, 1, n_tp)

    def raw_from(stage, s):
        return 0 if stage == 0 else 2 if goes_up(s) else 1

    def raw_copy(stage, s, other):
        i = raw_from(stage, s)
        source = (hand_b.at[i, s] if s < n_tp else hand_a.at[i, s - n_tp]) if other else blocks.at[i, s, 0]
        target = chip(1 if goes_up(s) == (stage == 0) else -1)
        return pltpu.make_async_remote_copy(
            src_ref=source,
            dst_ref=raw_in.at[stage, s, other],
            send_sem=raw_send.at[stage, s, other],
            recv_sem=raw_recv.at[stage, s, other],
            device_id={"expert": 2 * target + (1 - core if other else core)},
            device_id_type=MESH,
        )

    def raw_start(i, streams):
        for stage in range(2):
            chosen = [s for s in streams if raw_from(stage, s) == i]
            for s in chosen:
                for other in range(2):
                    raw_copy(stage, s, other).start()

    def raw_wait(stage, s):
        for other in range(2):
            pltpu.make_async_remote_copy(
                src_ref=raw_in.at[stage, s, other], dst_ref=raw_in.at[stage, s, other],
                send_sem=raw_send.at[stage, s, other], recv_sem=raw_recv.at[stage, s, other],
                device_id={"expert": partner}, device_id_type=MESH,
            ).wait_recv()

    def tok_copy(i, s, target):
        return pltpu.make_async_remote_copy(
            src_ref=tok.at[i - 1, s],
            dst_ref=tok_in.at[i - 1, s],
            send_sem=tok_send.at[i - 1, s],
            recv_sem=tok_recv.at[i - 1, s],
            device_id={"expert": 2 * target + core},
            device_id_type=MESH,
        )

    def left_rows(i):
        return h_buf[pl.ds(2 * i, 2)].reshape(2 * cap, h_buf.shape[2])

    def await_rows(i):
        for other in range(2):
            k = 2 * i + other
            pltpu.make_async_copy(hidden.at[0, 0], h_buf.at[k], h_sem.at[k]).wait()

    def product_early(i, r):
        product = jnp.dot(left_rows(i), w_early[r], preferred_element_type=f32)
        part[pl.ds(2 * i, 2), r] = product.astype(bf16).reshape(2, cap, TP_FIRST)

    def matmul_early(i, r):
        for way in range(n_tp - 1):
            @pl.when((i == 0) & (r == way + 1))
            def _():
                w_load(way + 1, True).wait()

        @pl.when(r == 0)
        def _():
            await_rows(i)

        product_early(i, r)
        for way in range(2):
            @pl.when(r == way)
            def _():
                ring_copy(i, way, 0).start()

    def product_late(i):
        product = jnp.dot(left_rows(i), w_late[...], preferred_element_type=f32).astype(bf16)
        for r in range(n_tp):
            piece = product[:, r * STREAM : (r + 1) * STREAM]
            blocks[i, r, 0] = piece[:cap]
            hand_b[i, r] = piece[cap:]

    def matmul_late(i, x):
        product_late(i)
        for begin in (1, 2):
            @pl.when(i == begin)
            def _():
                raw_start(begin, range(n_tp))

        hand_copy(i, False).start()

    def arrive(i, hop):
        for way in range(2):
            ring_copy(i, way, hop).wait_recv()
        for way in range(2):
            k, r = 2 * i + way, ring_part(way, hop + 1)
            part[k, r] = part[k, r] + ring_in[hop, k]
        for way in range(2):
            ring_copy(i, way, hop + 1).start()

    def arrive_last(i, x):
        hop = n_tp - 2
        for way in range(2):
            ring_copy(i, way, hop).wait_recv()
        for way in range(2):
            k = 2 * i + way
            for h in range(n_early):
                at = slice(h * STREAM, (h + 1) * STREAM)
                piece = part[k, n_tp - 1, :, at] + ring_in[hop, k, :, at]
                if way == 0:
                    blocks[i, n_tp + h, 0] = piece
                else:
                    hand_a[i, h] = piece

        for begin in range(3):
            @pl.when(i == begin)
            def _():
                raw_start(begin, range(n_tp, n_tp + n_early))

        @pl.when(i > 0)
        def _():
            hand_copy(i, True).start()

    def pick(j, rows):
        return jnp.dot(pick_hi[j], rows, preferred_element_type=f32) + jnp.dot(
            pick_lo[j], rows, preferred_element_type=f32
        )

    def weighted(i, s):
        return pick(i, blocks[i, s].reshape(2 * cap, STREAM))

    def chain(i, s):
        total = weighted(i, s)
        forward = (s < 2) | (s == n_tp)
        raw = (i == jnp.where(forward, 1, 2)) | (i == jnp.where(forward, 4, 3))

        @pl.when(raw)
        def _():
            stage = jnp.where(i > 2, 1, 0)
            raw_wait(stage, s)
            more = pick(jnp.where(i == 1, 0, i + LAST - 1), raw_in[stage, s].reshape(2 * cap, STREAM))
            tok[i - 1, s] = (total + more).astype(bf16)

        @pl.when(jnp.logical_not(raw))
        def _():
            tok_copy(i - 2, s, z).wait_recv()
            tok[i - 1, s] = (total + tok_in[i - 3, s].astype(f32)).astype(bf16)

        tok_copy(i, s, chip(jnp.where(lax.rem(i, 2) == 1, 1, -1))).start()

    def chain_first(i, s):
        @pl.when(s < n_tp)
        def _():
            hand_copy(i, False).wait_recv()

        @pl.when(s >= n_tp)
        def _():
            hand_copy(i, True).wait_recv()

        chain(i, s)

    def chain_end(s, total):
        for i in (LAST - 2, LAST - 1):
            tok_copy(i, s, z).wait_recv()
        return total + tok_in[LAST - 3, s].astype(f32) + tok_in[LAST - 2, s].astype(f32)

    def end_late(first, s):
        @pl.when(first == 1)
        def _():
            hand_copy(LAST, False).wait_recv()

        late[s] = chain_end(s, weighted(LAST, s)).astype(bf16)

    def late_step(i, x):
        @pl.when(x > 0)
        def _():
            for way in range(2):
                late_copy(way, x - 1).wait_recv()
            for way in range(2):
                here = pl.ds(way * half, half)
                r = ring_part(way, x)
                late[r, here] = late[r, here] + late_in[x - 1, way]

        for way in range(2):
            late_copy(way, x).start()

    def selection_table():
        rows = lax.broadcasted_iota(jnp.int32, (tokens, tokens), 0)
        cols = lax.broadcasted_iota(jnp.int32, (tokens, tokens), 1)
        earlier = jnp.where(rows < cols, 1.0, 0.0).astype(bf16)
        for j in range(1, LAST):
            for copy in route_copies(j):
                copy.wait_recv()
        for j, (group, shift) in enumerate(SETS):
            chosen, value = all_routes[group], all_scores[group]
            share = value / jnp.sum(value, axis=0, keepdims=True)
            for q in range(2):
                same = chosen == 2 * chip(shift) + (1 - core if q else core)
                line = 2 * j + q
                counts[line : line + 1, :] = jnp.sum(jnp.where(same, 1.0, 0.0), axis=0, keepdims=True)
                table[96 + line : 97 + line, :] = jnp.sum(jnp.where(same, share, 0.0), axis=0, keepdims=True)
        used = 2 * len(SETS)
        counts[used:, :] = jnp.zeros((counts.shape[0] - used, tokens), f32)
        table[96 + used :, :] = jnp.zeros((32 - used, tokens), f32)
        member = counts[...]
        before = jnp.dot(member.astype(bf16), earlier, preferred_element_type=f32)
        second = lax.rem(lax.broadcasted_iota(jnp.int32, member.shape, 0), 2) == 1
        portion = table[96:128, :]
        portion_hi = portion.astype(bf16).astype(f32)
        table[0:32, :] = jnp.where(member > 0.5, before + jnp.where(second, float(cap), 0.0), -1.0)
        table[32:64, :] = portion_hi
        table[64:96, :] = portion - portion_hi
        upright[...] = jnp.transpose(table[...])

    def selection_sets(sets):
        column = lax.broadcasted_iota(jnp.int32, (tokens, 2 * cap), 1).astype(f32)
        for j in sets:
            own, other = (column == upright[:, 2 * j + q : 2 * j + q + 1] for q in range(2))
            for target, base in ((pick_hi, 32), (pick_lo, 64)):
                a, b = (upright[:, base + 2 * j + q : base + 2 * j + q + 1] for q in range(2))
                target[j] = jnp.where(own, a, jnp.where(other, b, 0.0)).astype(bf16)

    def selection(i, x):
        pl.when(x == 0)(selection_table)
        for stage, sets in enumerate(((0, 8, 1, 2), (3, 4, 9, 10), (5, 6, 7))):
            @pl.when(x == stage + 1)
            def _():
                selection_sets(sets)

    def nothing(i, x):
        pass

    kinds = (
        matmul_early, matmul_late, arrive, chain, end_late, late_step, selection, arrive_last, chain_first,
        nothing,
    )

    await_rows(0)
    for r in range(n_tp):
        w_load(r, False).wait()
    product_late(0)
    w_load(0, True).wait()
    product_early(0, 0)
    pl.semaphore_wait(barrier, 2 + len(greeted))
    for i in range(1, LAST):
        for copy in route_copies(i):
            copy.start()
    raw_start(0, range(n_tp))
    ring_copy(0, 0, 0).start()
    all_routes[LAST] = routes[...]
    all_scores[LAST] = scores[...]

    def steps(j, carry):
        word = jnp.int32(WORDS[0])
        for n in range(1, len(WORDS)):
            word = jnp.where(j == n, WORDS[n], word)

        def step(m, inner):
            code = lax.rem(lax.shift_right_logical(word, 10 * m), 1024)
            i, x = lax.rem(code // 8, 8), lax.rem(code, 8)

            def branch(kind):
                def run():
                    kind(i, x)

                return run

            lax.switch(code // 64, [branch(kind) for kind in kinds])
            return inner

        lax.fori_loop(0, 3, step, 0)
        return carry

    lax.fori_loop(0, len(WORDS), steps, 0)

    for way in range(2):
        late_copy(way, n_tp - 2).wait_recv()
        here = slice(way * half, (way + 1) * half)
        mixed = late[n_tp - 1, here].astype(f32) + late_in[n_tp - 2, way].astype(f32)
        out[here, TP_FIRST:] = (residual[here, TP_FIRST:].astype(f32) + mixed).astype(bf16)
    hand_copy(LAST, True).wait_recv()
    totals = [weighted(LAST, n_tp + h) for h in range(n_early)]
    for h in range(n_early):
        at = slice(h * STREAM, (h + 1) * STREAM)
        out[:, at] = (residual[:, at].astype(f32) + chain_end(n_tp + h, totals[h])).astype(bf16)

    def drain(i, carry):
        for hop in range(n_tp - 1):
            for way in range(2):
                ring_copy(i, way, hop).wait_send()

        @pl.when(i > 0)
        def _():
            for early in (False, True):
                hand_copy(i, early).wait_send()

        @pl.when((i > 0) & (i < LAST))
        def _():
            for s in range(blocks.shape[1]):
                @pl.when(i != (2 if goes_up(s) else 1))
                def _():
                    tok_copy(i, s, z).wait_send()

        return carry

    lax.fori_loop(0, CHIPS, drain, 0)
    for stage in range(2):
        for s in range(blocks.shape[1]):
            for other in range(2):
                raw_copy(stage, s, other).wait_send()
    for i in range(1, LAST):
        for copy in route_copies(i):
            copy.wait_send()
    for hop in range(n_tp - 1):
        for way in range(2):
            late_copy(way, hop).wait_send()


def on_device(hidden, down_weight, routes, route_weight, residual):
    sources, cap, units = hidden.shape[1:]
    tokens, width = residual.shape
    top = routes.shape[1]
    n_tp = len(SLICE_SHIFT)
    early = TP_FIRST // STREAM
    streams = n_tp + early
    bf16, f32 = jnp.bfloat16, jnp.float32
    any_space = pl.BlockSpec(memory_space=pl.ANY)
    vmem = pl.BlockSpec(memory_space=pltpu.VMEM)
    dma = pltpu.SemaphoreType.DMA
    return pl.pallas_call(
        kernel,
        out_shape=jax.ShapeDtypeStruct((tokens, width), bf16),
        in_specs=[any_space, any_space, vmem, vmem, vmem],
        out_specs=vmem,
        scratch_shapes=[
            pltpu.VMEM((n_tp, units, TP_FIRST), bf16),
            pltpu.VMEM((units, n_tp * STREAM), bf16),
            pltpu.VMEM((sources, cap, units), bf16),
            pltpu.VMEM((sources, n_tp, cap, TP_FIRST), bf16),
            pltpu.VMEM((n_tp - 1, sources, cap, TP_FIRST), bf16),
            pltpu.VMEM((CHIPS, streams, 2, cap, STREAM), bf16),
            pltpu.VMEM((CHIPS, n_tp, cap, STREAM), bf16),
            pltpu.VMEM((CHIPS, early, cap, STREAM), bf16),
            pltpu.VMEM((2, streams, 2, cap, STREAM), bf16),
            pltpu.VMEM((LAST - 1, streams, tokens, STREAM), bf16),
            pltpu.VMEM((LAST - 1, streams, tokens, STREAM), bf16),
            pltpu.VMEM((n_tp, tokens, STREAM), bf16),
            pltpu.VMEM((n_tp - 1, 2, tokens // 2, STREAM), bf16),
            pltpu.VMEM((CHIPS, top, tokens), jnp.int32),
            pltpu.VMEM((CHIPS, top, tokens), f32),
            pltpu.VMEM((32, tokens), f32),
            pltpu.VMEM((128, tokens), f32),
            pltpu.VMEM((tokens, 128), f32),
            pltpu.VMEM((len(SETS), tokens, 2 * cap), bf16),
            pltpu.VMEM((len(SETS), tokens, 2 * cap), bf16),
            dma((n_tp,)),
            dma((n_tp,)),
            dma((sources,)),
            dma((n_tp - 1, sources)),
            dma((n_tp - 1, sources)),
            dma((CHIPS,)),
            dma((CHIPS,)),
            dma((CHIPS,)),
            dma((CHIPS,)),
            dma((2, streams, 2)),
            dma((2, streams, 2)),
            dma((LAST - 1, streams)),
            dma((LAST - 1, streams)),
            dma((n_tp - 1, 2)),
            dma((n_tp - 1, 2)),
            dma((LAST,)),
            dma((LAST,)),
            dma((LAST,)),
            dma((LAST,)),
        ],
        compiler_params=pltpu.CompilerParams(
            collective_id=0, has_side_effects=True, vmem_limit_bytes=60 * 1024 * 1024
        ),
        name="moe_down_combine",
    )(hidden, down_weight, routes.T, route_weight.T, residual)


def solution(mesh):
    return jax.shard_map(
        on_device,
        mesh=mesh,
        in_specs=(
            P("expert", "dp", None, "tp"),
            P("expert", "tp", None),
            P(("dp", "expert"), None),
            P(("dp", "expert"), None),
            P(("dp", "expert"), "tp"),
        ),
        out_specs=P(("dp", "expert"), "tp"),
        check_vma=False,
    )
```

```python
import jax
import jax.numpy as jnp
from jax import lax
from jax.experimental import pallas as pl
from jax.experimental.pallas import tpu as pltpu
from jax.sharding import PartitionSpec as P

MESH = pl.DeviceIdType.MESH

CHIPS = 8
LAST = CHIPS - 1
SLICE_SHIFT = (3, 1, 2, 0)
HOPS = ((0, 2, 1, 3), (1, 2, 0, 3))
TP_FIRST = 512
STREAM = 256

SETS = ((1, -1), (1, 0), (2, 0), (3, 0), (4, 0), (5, 0), (6, 0), (7, 0), (2, 1), (3, -1), (4, 1))

ORDER = (
    16, 8, 9, 72, 17, 80, 384, 2, 128, 385, 521, 32, 531, 33, 200, 10, 24, 88,
    136, 386, 210, 96, 129, 537, 48, 49, 547, 40, 219, 18, 25, 41, 3, 224, 144, 42,
    26, 216, 225, 218, 50, 34, 160, 450, 152, 226, 112, 387, 168, 104, 555, 137, 145, 27,
    560, 11, 243, 233, 153, 232, 19, 176, 161, 43, 241, 242, 458, 56, 466, 120, 234, 524,
    474, 35, 57, 267, 169, 541, 257, 177, 533, 256, 51, 258, 320, 482, 548, 220, 58, 490,
    229, 184, 557, 498, 321, 564, 236, 185, 245, 322, 59, 506,
)
FIRST_LOADS = ((False, (0, 2)), (True, (0, 1)), (False, (1, 3)), (True, (2, 3)))
ROW_ORDER = [code // 8 for code in ORDER if code < 64 and code % 8 == 0]
WORDS = tuple(
    sum(code << 10 * j for j, code in enumerate(ORDER[t : t + 3])) for t in range(0, len(ORDER), 3)
)


def kernel(
    hidden, weight, routes, scores, residual, out,
    w_early, w_late, h_buf, part, ring_in, blocks, hand_b, hand_a, raw_in, tok, tok_in, late, late_in,
    all_routes, all_scores, rest, staged, counts, table, upright, pick_hi, pick_lo,
    we_sem, wl_sem, h_sem, own_sem, out_sem, ring_send, ring_recv, hb_send, hb_recv, ha_send, ha_recv, raw_send, raw_recv,
    tok_send, tok_recv, late_send, late_recv, route_send, route_recv, score_send, score_recv,
):
    expert, tp = lax.axis_index("expert"), lax.axis_index("tp")
    n_tp = len(SLICE_SHIFT)
    n_early = TP_FIRST // STREAM
    cap, width = part.shape[2], residual.shape[1]
    tokens = residual.shape[0]
    half = tokens // 2
    f32, bf16 = jnp.float32, jnp.bfloat16
    z, core = expert // 2, lax.rem(expert, 2)
    up, down = lax.rem(tp + 1, n_tp), lax.rem(tp + n_tp - 1, n_tp)
    partner = 2 * z + 1 - core

    def chip(shift):
        return lax.rem(z + shift + CHIPS, CHIPS)

    def ahead(i):
        return (CHIPS // 2 - (i + 1) // 2) * (1 if i % 2 == 1 else -1)

    barrier = pltpu.get_barrier_semaphore()
    for peer in (up, down):
        pl.semaphore_signal(barrier, inc=1, device_id={"tp": peer}, device_id_type=MESH)
    greeted = [2 * chip(-ahead(i)) + core for i in range(1, LAST)]
    greeted += [partner, 2 * chip(1) + 1 - core, 2 * chip(-1) + 1 - core]
    for peer in greeted:
        pl.semaphore_signal(barrier, inc=1, device_id={"expert": peer}, device_id_type=MESH)

    def w_load(r, early):
        start = lax.rem(tp + SLICE_SHIFT[r], n_tp) * width
        if early:
            at = pl.ds(pl.multiple_of(start, STREAM), TP_FIRST)
            return pltpu.make_async_copy(weight.at[0, :, at], w_early.at[r], we_sem.at[r])
        at = pl.ds(pl.multiple_of(start + TP_FIRST, STREAM), STREAM)
        return pltpu.make_async_copy(
            weight.at[0, :, at], w_late.at[:, pl.ds(r * STREAM, STREAM)], wl_sem.at[r]
        )

    def h_load(i, other):
        source = 2 * chip(ahead(i)) + (1 - core if other else core)
        return pltpu.make_async_copy(hidden.at[0, source], h_buf.at[2 * i + other], h_sem.at[2 * i + other])

    for other in range(2):
        h_load(0, other).start()
    for early, rs in FIRST_LOADS:
        for r in rs:
            w_load(r, early).start()
    for i in ROW_ORDER:
        for other in range(2):
            h_load(i, other).start()

    own_copies = [
        pltpu.make_async_copy(routes, all_routes.at[LAST], own_sem.at[0]),
        pltpu.make_async_copy(scores, all_scores.at[LAST], own_sem.at[1]),
        pltpu.make_async_copy(residual, rest, own_sem.at[2]),
    ]
    for copy in own_copies:
        copy.start()

    def out_copy(j):
        at = pl.ds(j * STREAM, STREAM)
        return pltpu.make_async_copy(staged.at[:, at], out.at[:, at], out_sem.at[j])

    def route_copies(i):
        peer = {"expert": 2 * chip(-ahead(i)) + core}
        return [
            pltpu.make_async_remote_copy(
                src_ref=src, dst_ref=dst.at[i], send_sem=send.at[i], recv_sem=recv.at[i],
                device_id=peer, device_id_type=MESH,
            )
            for src, dst, send, recv in (
                (routes, all_routes, route_send, route_recv),
                (scores, all_scores, score_send, score_recv),
            )
        ]

    def ring_part(way, hop):
        first, second = HOPS[way][0], HOPS[way][2]
        return jnp.where(hop == 0, first, jnp.where(hop == 2, second, 2))

    def ring_copy(i, way, hop):
        k = 2 * i + way
        return pltpu.make_async_remote_copy(
            src_ref=part.at[k, ring_part(way, hop)],
            dst_ref=ring_in.at[hop, k],
            send_sem=ring_send.at[hop, k],
            recv_sem=ring_recv.at[hop, k],
            device_id={"tp": (up, down)[way]},
            device_id_type=MESH,
        )

    def late_copy(way, hop):
        return pltpu.make_async_remote_copy(
            src_ref=late.at[ring_part(way, hop), pl.ds(way * half, half)],
            dst_ref=late_in.at[hop, way],
            send_sem=late_send.at[hop, way],
            recv_sem=late_recv.at[hop, way],
            device_id={"tp": (up, down)[way]},
            device_id_type=MESH,
        )

    def hand_copy(i, early):
        first, count = (n_tp, n_early) if early else (0, n_tp)
        source, send, recv = (hand_a, ha_send, ha_recv) if early else (hand_b, hb_send, hb_recv)
        return pltpu.make_async_remote_copy(
            src_ref=source.at[i],
            dst_ref=blocks.at[i, pl.ds(first, count), 1],
            send_sem=send.at[i],
            recv_sem=recv.at[i],
            device_id={"expert": partner},
            device_id_type=MESH,
        )

    def goes_up(s):
        return s in (0, 1, n_tp)

    def raw_from(stage, s):
        return 0 if stage == 0 else 2 if goes_up(s) else 1

    def raw_copy(stage, s, other):
        i = raw_from(stage, s)
        source = (hand_b.at[i, s] if s < n_tp else hand_a.at[i, s - n_tp]) if other else blocks.at[i, s, 0]
        target = chip(1 if goes_up(s) == (stage == 0) else -1)
        return pltpu.make_async_remote_copy(
            src_ref=source,
            dst_ref=raw_in.at[stage, s, other],
            send_sem=raw_send.at[stage, s, other],
            recv_sem=raw_recv.at[stage, s, other],
            device_id={"expert": 2 * target + (1 - core if other else core)},
            device_id_type=MESH,
        )

    def raw_start(i, streams):
        for stage in range(2):
            chosen = [s for s in streams if raw_from(stage, s) == i]
            for s in chosen:
                for other in range(2):
                    raw_copy(stage, s, other).start()

    def raw_wait(stage, s):
        for other in range(2):
            pltpu.make_async_remote_copy(
                src_ref=raw_in.at[stage, s, other], dst_ref=raw_in.at[stage, s, other],
                send_sem=raw_send.at[stage, s, other], recv_sem=raw_recv.at[stage, s, other],
                device_id={"expert": partner}, device_id_type=MESH,
            ).wait_recv()

    def tok_copy(i, s, target):
        return pltpu.make_async_remote_copy(
            src_ref=tok.at[i - 1, s],
            dst_ref=tok_in.at[i - 1, s],
            send_sem=tok_send.at[i - 1, s],
            recv_sem=tok_recv.at[i - 1, s],
            device_id={"expert": 2 * target + core},
            device_id_type=MESH,
        )

    def left_rows(i):
        return h_buf[pl.ds(2 * i, 2)].reshape(2 * cap, h_buf.shape[2])

    def await_rows(i):
        for other in range(2):
            k = 2 * i + other
            pltpu.make_async_copy(hidden.at[0, 0], h_buf.at[k], h_sem.at[k]).wait()

    def product_early(i, r):
        product = jnp.dot(left_rows(i), w_early[r], preferred_element_type=f32)
        part[pl.ds(2 * i, 2), r] = product.astype(bf16).reshape(2, cap, TP_FIRST)

    def matmul_early(i, r):
        for new in (2, 3):
            @pl.when((i == 0) & (r == new))
            def _():
                w_load(new, True).wait()

        @pl.when(r == 0)
        def _():
            await_rows(i)

        product_early(i, r)
        for way in range(2):
            @pl.when(r == way)
            def _():
                ring_copy(i, way, 0).start()

    def product_late(i):
        product = jnp.dot(left_rows(i), w_late[...], preferred_element_type=f32).astype(bf16)
        for r in range(n_tp):
            piece = product[:, r * STREAM : (r + 1) * STREAM]
            blocks[i, r, 0] = piece[:cap]
            hand_b[i, r] = piece[cap:]

    def matmul_late(i, x):
        product_late(i)
        for begin in (1, 2):
            @pl.when(i == begin)
            def _():
                raw_start(begin, range(n_tp))

        hand_copy(i, False).start()

    def arrive(i, hop):
        for way in range(2):
            ring_copy(i, way, hop).wait_recv()
        for way in range(2):
            k, r = 2 * i + way, ring_part(way, hop + 1)
            part[k, r] = part[k, r] + ring_in[hop, k]
        for way in range(2):
            ring_copy(i, way, hop + 1).start()

    def arrive_last(i, x):
        hop = n_tp - 2
        for way in range(2):
            ring_copy(i, way, hop).wait_recv()
        for way in range(2):
            k = 2 * i + way
            for h in range(n_early):
                at = slice(h * STREAM, (h + 1) * STREAM)
                piece = part[k, n_tp - 1, :, at] + ring_in[hop, k, :, at]
                if way == 0:
                    blocks[i, n_tp + h, 0] = piece
                else:
                    hand_a[i, h] = piece

        for begin in range(3):
            @pl.when(i == begin)
            def _():
                raw_start(begin, range(n_tp, n_tp + n_early))

        @pl.when(i > 0)
        def _():
            hand_copy(i, True).start()

    def pick(j, rows):
        return jnp.dot(pick_hi[j], rows, preferred_element_type=f32) + jnp.dot(
            pick_lo[j], rows, preferred_element_type=f32
        )

    def weighted(i, s):
        return pick(i, blocks[i, s].reshape(2 * cap, STREAM))

    def chain(i, s):
        total = weighted(i, s)
        forward = (s < 2) | (s == n_tp)
        raw = (i == jnp.where(forward, 1, 2)) | (i == jnp.where(forward, 4, 3))

        @pl.when(raw)
        def _():
            stage = jnp.where(i > 2, 1, 0)
            raw_wait(stage, s)
            more = pick(jnp.where(i == 1, 0, i + LAST - 1), raw_in[stage, s].reshape(2 * cap, STREAM))
            tok[i - 1, s] = (total + more).astype(bf16)

        @pl.when(jnp.logical_not(raw))
        def _():
            tok_copy(i - 2, s, z).wait_recv()
            tok[i - 1, s] = (total + tok_in[i - 3, s].astype(f32)).astype(bf16)

        tok_copy(i, s, chip(jnp.where(lax.rem(i, 2) == 1, 1, -1))).start()

    def chain_first(i, s):
        @pl.when(s < n_tp)
        def _():
            hand_copy(i, False).wait_recv()

        @pl.when(s >= n_tp)
        def _():
            hand_copy(i, True).wait_recv()

        chain(i, s)

    def chain_end(s, total):
        for i in (LAST - 2, LAST - 1):
            tok_copy(i, s, z).wait_recv()
        return total + tok_in[LAST - 3, s].astype(f32) + tok_in[LAST - 2, s].astype(f32)

    def end_late(first, s):
        @pl.when(first == 1)
        def _():
            hand_copy(LAST, False).wait_recv()

        late[s] = chain_end(s, weighted(LAST, s)).astype(bf16)

    def late_step(i, x):
        @pl.when(x > 0)
        def _():
            for way in range(2):
                late_copy(way, x - 1).wait_recv()
            for way in range(2):
                here = pl.ds(way * half, half)
                r = ring_part(way, x)
                late[r, here] = late[r, here] + late_in[x - 1, way]

        for way in range(2):
            late_copy(way, x).start()

    def selection_table():
        rows = lax.broadcasted_iota(jnp.int32, (tokens, tokens), 0)
        cols = lax.broadcasted_iota(jnp.int32, (tokens, tokens), 1)
        earlier = jnp.where(rows < cols, 1.0, 0.0).astype(bf16)
        for j in range(1, LAST):
            for copy in route_copies(j):
                copy.wait_recv()
        for copy in own_copies[:2]:
            copy.wait()
        for j, (group, shift) in enumerate(SETS):
            chosen, value = all_routes[group], all_scores[group]
            share = value / jnp.sum(value, axis=0, keepdims=True)
            for q in range(2):
                same = chosen == 2 * chip(shift) + (1 - core if q else core)
                line = 2 * j + q
                counts[line : line + 1, :] = jnp.sum(jnp.where(same, 1.0, 0.0), axis=0, keepdims=True)
                table[96 + line : 97 + line, :] = jnp.sum(jnp.where(same, share, 0.0), axis=0, keepdims=True)
        used = 2 * len(SETS)
        counts[used:, :] = jnp.zeros((counts.shape[0] - used, tokens), f32)
        table[96 + used :, :] = jnp.zeros((32 - used, tokens), f32)
        member = counts[...]
        before = jnp.dot(member.astype(bf16), earlier, preferred_element_type=f32)
        second = lax.rem(lax.broadcasted_iota(jnp.int32, member.shape, 0), 2) == 1
        portion = table[96:128, :]
        portion_hi = portion.astype(bf16).astype(f32)
        table[0:32, :] = jnp.where(member > 0.5, before + jnp.where(second, float(cap), 0.0), -1.0)
        table[32:64, :] = portion_hi
        table[64:96, :] = portion - portion_hi
        upright[...] = jnp.transpose(table[...])

    def selection_sets(sets):
        column = lax.broadcasted_iota(jnp.int32, (tokens, 2 * cap), 1).astype(f32)
        for j in sets:
            own, other = (column == upright[:, 2 * j + q : 2 * j + q + 1] for q in range(2))
            for target, base in ((pick_hi, 32), (pick_lo, 64)):
                a, b = (upright[:, base + 2 * j + q : base + 2 * j + q + 1] for q in range(2))
                target[j] = jnp.where(own, a, jnp.where(other, b, 0.0)).astype(bf16)

    def selection(i, x):
        pl.when(x == 0)(selection_table)
        for stage, sets in enumerate(((0, 8, 1, 2), (3, 4, 9, 10), (5, 6, 7))):
            @pl.when(x == stage + 1)
            def _():
                selection_sets(sets)

    def nothing(i, x):
        pass

    kinds = (
        matmul_early, matmul_late, arrive, chain, end_late, late_step, selection, arrive_last, chain_first,
        nothing,
    )

    def first_late(r):
        w_load(r, False).wait()
        at = slice(r * STREAM, (r + 1) * STREAM)
        product = jnp.dot(left_rows(0), w_late[:, at], preferred_element_type=f32).astype(bf16)
        blocks[0, r, 0] = product[:cap]
        hand_b[0, r] = product[cap:]

    await_rows(0)
    first_late(0)
    pl.semaphore_wait(barrier, 2 + len(greeted))
    for i in range(1, LAST):
        for copy in route_copies(i):
            copy.start()
    raw_start(0, (0,))
    first_late(2)
    raw_start(0, (2,))
    for way in range(2):
        w_load(way, True).wait()
        product_early(0, way)
        ring_copy(0, way, 0).start()
    for r in (1, 3):
        first_late(r)
        raw_start(0, (r,))

    def steps(j, carry):
        word = jnp.int32(WORDS[0])
        for n in range(1, len(WORDS)):
            word = jnp.where(j == n, WORDS[n], word)

        def step(m, inner):
            code = lax.rem(lax.shift_right_logical(word, 10 * m), 1024)
            i, x = lax.rem(code // 8, 8), lax.rem(code, 8)

            def branch(kind):
                def run():
                    kind(i, x)

                return run

            lax.switch(code // 64, [branch(kind) for kind in kinds])
            return inner

        lax.fori_loop(0, 3, step, 0)
        return carry

    lax.fori_loop(0, len(WORDS), steps, 0)

    own_copies[2].wait()
    for way in range(2):
        late_copy(way, n_tp - 2).wait_recv()
        here = slice(way * half, (way + 1) * half)
        mixed = late[n_tp - 1, here].astype(f32) + late_in[n_tp - 2, way].astype(f32)
        staged[here, TP_FIRST:] = (rest[here, TP_FIRST:].astype(f32) + mixed).astype(bf16)
    out_copy(n_early).start()
    hand_copy(LAST, True).wait_recv()
    totals = []
    for h in range(n_early):
        at = slice(h * STREAM, (h + 1) * STREAM)
        totals.append(rest[:, at].astype(f32) + weighted(LAST, n_tp + h))
    for h in range(n_early):
        staged[:, h * STREAM : (h + 1) * STREAM] = chain_end(n_tp + h, totals[h]).astype(bf16)
        out_copy(h).start()

    def drain(i, carry):
        for hop in range(n_tp - 1):
            for way in range(2):
                ring_copy(i, way, hop).wait_send()

        @pl.when(i > 0)
        def _():
            for early in (False, True):
                hand_copy(i, early).wait_send()

        @pl.when((i > 0) & (i < LAST))
        def _():
            for s in range(blocks.shape[1]):
                @pl.when(i != (2 if goes_up(s) else 1))
                def _():
                    tok_copy(i, s, z).wait_send()

        return carry

    lax.fori_loop(0, CHIPS, drain, 0)
    for j in range(n_early + 1):
        out_copy(j).wait()
    for stage in range(2):
        for s in range(blocks.shape[1]):
            for other in range(2):
                raw_copy(stage, s, other).wait_send()
    for i in range(1, LAST):
        for copy in route_copies(i):
            copy.wait_send()
    for hop in range(n_tp - 1):
        for way in range(2):
            late_copy(way, hop).wait_send()


def on_device(hidden, down_weight, routes, route_weight, residual):
    sources, cap, units = hidden.shape[1:]
    tokens, width = residual.shape
    top = routes.shape[1]
    n_tp = len(SLICE_SHIFT)
    early = TP_FIRST // STREAM
    streams = n_tp + early
    bf16, f32 = jnp.bfloat16, jnp.float32
    any_space = pl.BlockSpec(memory_space=pl.ANY)
    dma = pltpu.SemaphoreType.DMA
    return pl.pallas_call(
        kernel,
        out_shape=jax.ShapeDtypeStruct((tokens, width), bf16),
        in_specs=[any_space] * 5,
        out_specs=any_space,
        scratch_shapes=[
            pltpu.VMEM((n_tp, units, TP_FIRST), bf16),
            pltpu.VMEM((units, n_tp * STREAM), bf16),
            pltpu.VMEM((sources, cap, units), bf16),
            pltpu.VMEM((sources, n_tp, cap, TP_FIRST), bf16),
            pltpu.VMEM((n_tp - 1, sources, cap, TP_FIRST), bf16),
            pltpu.VMEM((CHIPS, streams, 2, cap, STREAM), bf16),
            pltpu.VMEM((CHIPS, n_tp, cap, STREAM), bf16),
            pltpu.VMEM((CHIPS, early, cap, STREAM), bf16),
            pltpu.VMEM((2, streams, 2, cap, STREAM), bf16),
            pltpu.VMEM((LAST - 1, streams, tokens, STREAM), bf16),
            pltpu.VMEM((LAST - 1, streams, tokens, STREAM), bf16),
            pltpu.VMEM((n_tp, tokens, STREAM), bf16),
            pltpu.VMEM((n_tp - 1, 2, tokens // 2, STREAM), bf16),
            pltpu.VMEM((CHIPS, top, tokens), jnp.int32),
            pltpu.VMEM((CHIPS, top, tokens), f32),
            pltpu.VMEM((tokens, width), bf16),
            pltpu.VMEM((tokens, width), bf16),
            pltpu.VMEM((32, tokens), f32),
            pltpu.VMEM((128, tokens), f32),
            pltpu.VMEM((tokens, 128), f32),
            pltpu.VMEM((len(SETS), tokens, 2 * cap), bf16),
            pltpu.VMEM((len(SETS), tokens, 2 * cap), bf16),
            dma((n_tp,)),
            dma((n_tp,)),
            dma((sources,)),
            dma((3,)),
            dma((early + 1,)),
            dma((n_tp - 1, sources)),
            dma((n_tp - 1, sources)),
            dma((CHIPS,)),
            dma((CHIPS,)),
            dma((CHIPS,)),
            dma((CHIPS,)),
            dma((2, streams, 2)),
            dma((2, streams, 2)),
            dma((LAST - 1, streams)),
            dma((LAST - 1, streams)),
            dma((n_tp - 1, 2)),
            dma((n_tp - 1, 2)),
            dma((LAST,)),
            dma((LAST,)),
            dma((LAST,)),
            dma((LAST,)),
        ],
        compiler_params=pltpu.CompilerParams(
            collective_id=0, has_side_effects=True, vmem_limit_bytes=60 * 1024 * 1024
        ),
        name="moe_down_combine",
    )(hidden, down_weight, routes.T, route_weight.T, residual)


def solution(mesh):
    return jax.shard_map(
        on_device,
        mesh=mesh,
        in_specs=(
            P("expert", "dp", None, "tp"),
            P("expert", "tp", None),
            P(("dp", "expert"), None),
            P(("dp", "expert"), None),
            P(("dp", "expert"), "tp"),
        ),
        out_specs=P(("dp", "expert"), "tp"),
        check_vma=False,
    )
```

```python
import jax
import jax.numpy as jnp
from jax import lax
from jax.experimental import pallas as pl
from jax.experimental.pallas import tpu as pltpu
from jax.sharding import PartitionSpec as P

MESH = pl.DeviceIdType.MESH

CHIPS = 8
LAST = CHIPS - 1
SLICE_SHIFT = (3, 1, 2, 0)
HOPS = ((0, 2, 1, 3), (1, 2, 0, 3))
TP_FIRST = 512
STREAM = 256

SETS = ((1, -1), (1, 0), (2, 0), (3, 0), (4, 0), (5, 0), (6, 0), (7, 0), (2, 1), (3, -1), (4, 1))

ORDER = (
    16, 2, 17, 8, 72, 9, 80, 128, 24, 384, 385, 25, 10, 520, 531, 88, 136, 32,
    210, 96, 201, 129, 386, 545, 539, 218, 33, 18, 227, 144, 40, 3, 387, 41, 48, 217,
    34, 226, 216, 104, 160, 112, 137, 42, 224, 26, 49, 554, 450, 235, 152, 11, 35, 168,
    233, 562, 27, 243, 240, 50, 145, 153, 458, 176, 161, 232, 241, 169, 56, 524, 57, 120,
    19, 267, 474, 466, 533, 541, 177, 258, 482, 257, 51, 256, 320, 58, 548, 43, 220, 490,
    59, 184, 229, 498, 557, 321, 564, 185, 236, 245, 322, 506,
)
FIRST_LOADS = ((False, (0, 2)), (True, (0, 1)), (False, (1, 3)), (True, (2, 3)))
ROW_ORDER = [code // 8 for code in ORDER if code < 64 and code % 8 == 0]
WORDS = tuple(
    sum(code << 10 * j for j, code in enumerate(ORDER[t : t + 3])) for t in range(0, len(ORDER), 3)
)


def kernel(
    hidden, weight, routes, scores, residual, out,
    w_early, w_late, h_buf, part, ring_in, blocks, hand_b, hand_a, raw_in, tok, tok_in, late, late_in,
    all_routes, all_scores, rest, counts, table, upright, pick_hi, pick_lo,
    we_sem, wl_sem, h_sem, own_sem, ring_send, ring_recv, hb_send, hb_recv, ha_send, ha_recv, raw_send, raw_recv,
    tok_send, tok_recv, late_send, late_recv, route_send, route_recv, score_send, score_recv,
):
    expert, tp = lax.axis_index("expert"), lax.axis_index("tp")
    n_tp = len(SLICE_SHIFT)
    n_early = TP_FIRST // STREAM
    cap, width = part.shape[2], residual.shape[1]
    tokens = residual.shape[0]
    half = tokens // 2
    f32, bf16 = jnp.float32, jnp.bfloat16
    z, core = expert // 2, lax.rem(expert, 2)
    up, down = lax.rem(tp + 1, n_tp), lax.rem(tp + n_tp - 1, n_tp)
    partner = 2 * z + 1 - core

    def chip(shift):
        return lax.rem(z + shift + CHIPS, CHIPS)

    def ahead(i):
        return (CHIPS // 2 - (i + 1) // 2) * (1 if i % 2 == 1 else -1)

    def w_load(r, early):
        start = lax.rem(tp + SLICE_SHIFT[r], n_tp) * width
        if early:
            at = pl.ds(pl.multiple_of(start, STREAM), TP_FIRST)
            return pltpu.make_async_copy(weight.at[0, :, at], w_early.at[r], we_sem.at[r])
        at = pl.ds(pl.multiple_of(start + TP_FIRST, STREAM), STREAM)
        return pltpu.make_async_copy(
            weight.at[0, :, at], w_late.at[:, pl.ds(r * STREAM, STREAM)], wl_sem.at[r]
        )

    def h_load(i, other):
        source = 2 * chip(ahead(i)) + (1 - core if other else core)
        return pltpu.make_async_copy(hidden.at[0, source], h_buf.at[2 * i + other], h_sem.at[2 * i + other])

    for other in range(2):
        h_load(0, other).start()
    early, rs = FIRST_LOADS[0]
    for r in rs:
        w_load(r, early).start()

    barrier = pltpu.get_barrier_semaphore()
    for peer in (up, down):
        pl.semaphore_signal(barrier, inc=1, device_id={"tp": peer}, device_id_type=MESH)
    greeted = [2 * chip(-ahead(i)) + core for i in range(1, LAST)]
    greeted += [partner, 2 * chip(1) + 1 - core, 2 * chip(-1) + 1 - core]
    for peer in greeted:
        pl.semaphore_signal(barrier, inc=1, device_id={"expert": peer}, device_id_type=MESH)

    for early, rs in FIRST_LOADS[1:]:
        for r in rs:
            w_load(r, early).start()
    for i in ROW_ORDER:
        for other in range(2):
            h_load(i, other).start()

    own_copies = [
        pltpu.make_async_copy(routes, all_routes.at[LAST], own_sem.at[0]),
        pltpu.make_async_copy(scores, all_scores.at[LAST], own_sem.at[1]),
        pltpu.make_async_copy(residual, rest, own_sem.at[2]),
    ]
    for copy in own_copies:
        copy.start()

    def route_copies(i):
        peer = {"expert": 2 * chip(-ahead(i)) + core}
        return [
            pltpu.make_async_remote_copy(
                src_ref=src, dst_ref=dst.at[i], send_sem=send.at[i], recv_sem=recv.at[i],
                device_id=peer, device_id_type=MESH,
            )
            for src, dst, send, recv in (
                (routes, all_routes, route_send, route_recv),
                (scores, all_scores, score_send, score_recv),
            )
        ]

    def ring_part(way, hop):
        first, second = HOPS[way][0], HOPS[way][2]
        return jnp.where(hop == 0, first, jnp.where(hop == 2, second, 2))

    def ring_copy(i, way, hop):
        k = 2 * i + way
        return pltpu.make_async_remote_copy(
            src_ref=part.at[k, ring_part(way, hop)],
            dst_ref=ring_in.at[hop, k],
            send_sem=ring_send.at[hop, k],
            recv_sem=ring_recv.at[hop, k],
            device_id={"tp": (up, down)[way]},
            device_id_type=MESH,
        )

    def late_copy(way, hop):
        return pltpu.make_async_remote_copy(
            src_ref=late.at[ring_part(way, hop), pl.ds(way * half, half)],
            dst_ref=late_in.at[hop, way],
            send_sem=late_send.at[hop, way],
            recv_sem=late_recv.at[hop, way],
            device_id={"tp": (up, down)[way]},
            device_id_type=MESH,
        )

    def hand_copy(i, early):
        first, count = (n_tp, n_early) if early else (0, n_tp)
        source, send, recv = (hand_a, ha_send, ha_recv) if early else (hand_b, hb_send, hb_recv)
        return pltpu.make_async_remote_copy(
            src_ref=source.at[i],
            dst_ref=blocks.at[i, pl.ds(first, count), 1],
            send_sem=send.at[i],
            recv_sem=recv.at[i],
            device_id={"expert": partner},
            device_id_type=MESH,
        )

    def goes_up(s):
        return s in (0, 1, n_tp)

    def raw_from(stage, s):
        return 0 if stage == 0 else 2 if goes_up(s) else 1

    def raw_copy(stage, s, other):
        i = raw_from(stage, s)
        source = (hand_b.at[i, s] if s < n_tp else hand_a.at[i, s - n_tp]) if other else blocks.at[i, s, 0]
        target = chip(1 if goes_up(s) == (stage == 0) else -1)
        return pltpu.make_async_remote_copy(
            src_ref=source,
            dst_ref=raw_in.at[stage, s, other],
            send_sem=raw_send.at[stage, s, other],
            recv_sem=raw_recv.at[stage, s, other],
            device_id={"expert": 2 * target + (1 - core if other else core)},
            device_id_type=MESH,
        )

    def raw_start(i, streams):
        for stage in range(2):
            chosen = [s for s in streams if raw_from(stage, s) == i]
            for s in chosen:
                for other in range(2):
                    raw_copy(stage, s, other).start()

    def raw_wait(stage, s):
        for other in range(2):
            pltpu.make_async_remote_copy(
                src_ref=raw_in.at[stage, s, other], dst_ref=raw_in.at[stage, s, other],
                send_sem=raw_send.at[stage, s, other], recv_sem=raw_recv.at[stage, s, other],
                device_id={"expert": partner}, device_id_type=MESH,
            ).wait_recv()

    def tok_copy(i, s, target):
        return pltpu.make_async_remote_copy(
            src_ref=tok.at[i - 1, s],
            dst_ref=tok_in.at[i - 1, s],
            send_sem=tok_send.at[i - 1, s],
            recv_sem=tok_recv.at[i - 1, s],
            device_id={"expert": 2 * target + core},
            device_id_type=MESH,
        )

    def left_rows(i):
        return h_buf[pl.ds(2 * i, 2)].reshape(2 * cap, h_buf.shape[2])

    def await_rows(i):
        for other in range(2):
            k = 2 * i + other
            pltpu.make_async_copy(hidden.at[0, 0], h_buf.at[k], h_sem.at[k]).wait()

    def product_early(i, r):
        product = jnp.dot(left_rows(i), w_early[r], preferred_element_type=f32)
        part[pl.ds(2 * i, 2), r] = product.astype(bf16).reshape(2, cap, TP_FIRST)

    def matmul_early(i, r):
        for new in (2, 3):
            @pl.when((i == 0) & (r == new))
            def _():
                w_load(new, True).wait()

        @pl.when(r == 0)
        def _():
            await_rows(i)

        product_early(i, r)
        for way in range(2):
            @pl.when(r == way)
            def _():
                ring_copy(i, way, 0).start()

    def product_late(i):
        product = jnp.dot(left_rows(i), w_late[...], preferred_element_type=f32).astype(bf16)
        for r in range(n_tp):
            piece = product[:, r * STREAM : (r + 1) * STREAM]
            blocks[i, r, 0] = piece[:cap]
            hand_b[i, r] = piece[cap:]

    def matmul_late(i, x):
        product_late(i)
        for begin in (1, 2):
            @pl.when(i == begin)
            def _():
                raw_start(begin, range(n_tp))

        hand_copy(i, False).start()

    def arrive(i, hop):
        for way in range(2):
            ring_copy(i, way, hop).wait_recv()
        for way in range(2):
            k, r = 2 * i + way, ring_part(way, hop + 1)
            part[k, r] = part[k, r] + ring_in[hop, k]
        for way in range(2):
            ring_copy(i, way, hop + 1).start()

    def arrive_last(i, x):
        hop = n_tp - 2
        for way in range(2):
            ring_copy(i, way, hop).wait_recv()
        for way in range(2):
            k = 2 * i + way
            for h in range(n_early):
                at = slice(h * STREAM, (h + 1) * STREAM)
                piece = part[k, n_tp - 1, :, at] + ring_in[hop, k, :, at]
                if way == 0:
                    blocks[i, n_tp + h, 0] = piece
                else:
                    hand_a[i, h] = piece

        for begin in range(3):
            @pl.when(i == begin)
            def _():
                raw_start(begin, range(n_tp, n_tp + n_early))

        @pl.when(i > 0)
        def _():
            hand_copy(i, True).start()

    def pick(j, rows):
        return jnp.dot(pick_hi[j], rows, preferred_element_type=f32) + jnp.dot(
            pick_lo[j], rows, preferred_element_type=f32
        )

    def weighted(i, s):
        return pick(i, blocks[i, s].reshape(2 * cap, STREAM))

    def chain(i, s):
        total = weighted(i, s)
        forward = (s < 2) | (s == n_tp)
        raw = (i == jnp.where(forward, 1, 2)) | (i == jnp.where(forward, 4, 3))

        @pl.when(raw)
        def _():
            stage = jnp.where(i > 2, 1, 0)
            raw_wait(stage, s)
            more = pick(jnp.where(i == 1, 0, i + LAST - 1), raw_in[stage, s].reshape(2 * cap, STREAM))
            tok[i - 1, s] = (total + more).astype(bf16)

        @pl.when(jnp.logical_not(raw))
        def _():
            tok_copy(i - 2, s, z).wait_recv()
            tok[i - 1, s] = (total + tok_in[i - 3, s].astype(f32)).astype(bf16)

        tok_copy(i, s, chip(jnp.where(lax.rem(i, 2) == 1, 1, -1))).start()

    def chain_first(i, s):
        @pl.when(s < n_tp)
        def _():
            hand_copy(i, False).wait_recv()

        @pl.when(s >= n_tp)
        def _():
            hand_copy(i, True).wait_recv()

        chain(i, s)

    def chain_end(s, total):
        for i in (LAST - 2, LAST - 1):
            tok_copy(i, s, z).wait_recv()
        return total + tok_in[LAST - 3, s].astype(f32) + tok_in[LAST - 2, s].astype(f32)

    def end_late(first, s):
        @pl.when(first == 1)
        def _():
            hand_copy(LAST, False).wait_recv()

        late[s] = chain_end(s, weighted(LAST, s)).astype(bf16)

    def late_step(i, x):
        @pl.when(x > 0)
        def _():
            for way in range(2):
                late_copy(way, x - 1).wait_recv()
            for way in range(2):
                here = pl.ds(way * half, half)
                r = ring_part(way, x)
                late[r, here] = late[r, here] + late_in[x - 1, way]

        for way in range(2):
            late_copy(way, x).start()

    def selection_table():
        rows = lax.broadcasted_iota(jnp.int32, (tokens, tokens), 0)
        cols = lax.broadcasted_iota(jnp.int32, (tokens, tokens), 1)
        earlier = jnp.where(rows < cols, 1.0, 0.0).astype(bf16)
        for j in range(1, LAST):
            for copy in route_copies(j):
                copy.wait_recv()
        for copy in own_copies[:2]:
            copy.wait()
        for j, (group, shift) in enumerate(SETS):
            chosen, value = all_routes[group], all_scores[group]
            share = value / jnp.sum(value, axis=0, keepdims=True)
            for q in range(2):
                same = chosen == 2 * chip(shift) + (1 - core if q else core)
                line = 2 * j + q
                counts[line : line + 1, :] = jnp.sum(jnp.where(same, 1.0, 0.0), axis=0, keepdims=True)
                table[96 + line : 97 + line, :] = jnp.sum(jnp.where(same, share, 0.0), axis=0, keepdims=True)
        used = 2 * len(SETS)
        counts[used:, :] = jnp.zeros((counts.shape[0] - used, tokens), f32)
        table[96 + used :, :] = jnp.zeros((32 - used, tokens), f32)
        member = counts[...]
        before = jnp.dot(member.astype(bf16), earlier, preferred_element_type=f32)
        second = lax.rem(lax.broadcasted_iota(jnp.int32, member.shape, 0), 2) == 1
        portion = table[96:128, :]
        portion_hi = portion.astype(bf16).astype(f32)
        table[0:32, :] = jnp.where(member > 0.5, before + jnp.where(second, float(cap), 0.0), -1.0)
        table[32:64, :] = portion_hi
        table[64:96, :] = portion - portion_hi
        upright[...] = jnp.transpose(table[...])

    def selection_sets(sets):
        column = lax.broadcasted_iota(jnp.int32, (tokens, 2 * cap), 1).astype(f32)
        for j in sets:
            own, other = (column == upright[:, 2 * j + q : 2 * j + q + 1] for q in range(2))
            for target, base in ((pick_hi, 32), (pick_lo, 64)):
                a, b = (upright[:, base + 2 * j + q : base + 2 * j + q + 1] for q in range(2))
                target[j] = jnp.where(own, a, jnp.where(other, b, 0.0)).astype(bf16)

    def selection(i, x):
        pl.when(x == 0)(selection_table)
        for stage, sets in enumerate(((0, 8, 1, 2), (3, 4, 9, 10), (5, 6, 7))):
            @pl.when(x == stage + 1)
            def _():
                selection_sets(sets)

    def nothing(i, x):
        pass

    kinds = (
        matmul_early, matmul_late, arrive, chain, end_late, late_step, selection, arrive_last, chain_first,
        nothing,
    )

    def first_late(r):
        w_load(r, False).wait()
        at = slice(r * STREAM, (r + 1) * STREAM)
        product = jnp.dot(left_rows(0), w_late[:, at], preferred_element_type=f32).astype(bf16)
        blocks[0, r, 0] = product[:cap]
        hand_b[0, r] = product[cap:]

    await_rows(0)
    first_late(0)
    pl.semaphore_wait(barrier, 2 + len(greeted))
    for i in range(1, LAST):
        for copy in route_copies(i):
            copy.start()
    raw_start(0, (0,))
    first_late(2)
    raw_start(0, (2,))
    for way in range(2):
        w_load(way, True).wait()
        product_early(0, way)
        ring_copy(0, way, 0).start()
    for r in (1, 3):
        first_late(r)
        raw_start(0, (r,))

    def steps(j, carry):
        word = jnp.int32(WORDS[0])
        for n in range(1, len(WORDS)):
            word = jnp.where(j == n, WORDS[n], word)

        def step(m, inner):
            code = lax.rem(lax.shift_right_logical(word, 10 * m), 1024)
            i, x = lax.rem(code // 8, 8), lax.rem(code, 8)

            def branch(kind):
                def run():
                    kind(i, x)

                return run

            lax.switch(code // 64, [branch(kind) for kind in kinds])
            return inner

        lax.fori_loop(0, 3, step, 0)
        return carry

    lax.fori_loop(0, len(WORDS), steps, 0)

    own_copies[2].wait()
    for way in range(2):
        late_copy(way, n_tp - 2).wait_recv()
        here = slice(way * half, (way + 1) * half)
        mixed = late[n_tp - 1, here].astype(f32) + late_in[n_tp - 2, way].astype(f32)
        out[here, TP_FIRST:] = (rest[here, TP_FIRST:].astype(f32) + mixed).astype(bf16)
    hand_copy(LAST, True).wait_recv()
    totals = []
    for h in range(n_early):
        at = slice(h * STREAM, (h + 1) * STREAM)
        totals.append(rest[:, at].astype(f32) + weighted(LAST, n_tp + h))
    for h in range(n_early):
        out[:, h * STREAM : (h + 1) * STREAM] = chain_end(n_tp + h, totals[h]).astype(bf16)

    def drain(i, carry):
        for hop in range(n_tp - 1):
            for way in range(2):
                ring_copy(i, way, hop).wait_send()

        @pl.when(i > 0)
        def _():
            for early in (False, True):
                hand_copy(i, early).wait_send()

        @pl.when((i > 0) & (i < LAST))
        def _():
            for s in range(blocks.shape[1]):
                @pl.when(i != (2 if goes_up(s) else 1))
                def _():
                    tok_copy(i, s, z).wait_send()

        return carry

    lax.fori_loop(0, CHIPS, drain, 0)
    for stage in range(2):
        for s in range(blocks.shape[1]):
            for other in range(2):
                raw_copy(stage, s, other).wait_send()
    for i in range(1, LAST):
        for copy in route_copies(i):
            copy.wait_send()
    for hop in range(n_tp - 1):
        for way in range(2):
            late_copy(way, hop).wait_send()


def on_device(hidden, down_weight, routes, route_weight, residual):
    sources, cap, units = hidden.shape[1:]
    tokens, width = residual.shape
    top = routes.shape[1]
    n_tp = len(SLICE_SHIFT)
    early = TP_FIRST // STREAM
    streams = n_tp + early
    bf16, f32 = jnp.bfloat16, jnp.float32
    any_space = pl.BlockSpec(memory_space=pl.ANY)
    dma = pltpu.SemaphoreType.DMA
    return pl.pallas_call(
        kernel,
        out_shape=pltpu.VMEM((tokens, width), bf16),
        in_specs=[any_space] * 5,
        out_specs=pl.BlockSpec(memory_space=pltpu.VMEM),
        scratch_shapes=[
            pltpu.VMEM((n_tp, units, TP_FIRST), bf16),
            pltpu.VMEM((units, n_tp * STREAM), bf16),
            pltpu.VMEM((sources, cap, units), bf16),
            pltpu.VMEM((sources, n_tp, cap, TP_FIRST), bf16),
            pltpu.VMEM((n_tp - 1, sources, cap, TP_FIRST), bf16),
            pltpu.VMEM((CHIPS, streams, 2, cap, STREAM), bf16),
            pltpu.VMEM((CHIPS, n_tp, cap, STREAM), bf16),
            pltpu.VMEM((CHIPS, early, cap, STREAM), bf16),
            pltpu.VMEM((2, streams, 2, cap, STREAM), bf16),
            pltpu.VMEM((LAST - 1, streams, tokens, STREAM), bf16),
            pltpu.VMEM((LAST - 1, streams, tokens, STREAM), bf16),
            pltpu.VMEM((n_tp, tokens, STREAM), bf16),
            pltpu.VMEM((n_tp - 1, 2, tokens // 2, STREAM), bf16),
            pltpu.VMEM((CHIPS, top, tokens), jnp.int32),
            pltpu.VMEM((CHIPS, top, tokens), f32),
            pltpu.VMEM((tokens, width), bf16),
            pltpu.VMEM((32, tokens), f32),
            pltpu.VMEM((128, tokens), f32),
            pltpu.VMEM((tokens, 128), f32),
            pltpu.VMEM((len(SETS), tokens, 2 * cap), bf16),
            pltpu.VMEM((len(SETS), tokens, 2 * cap), bf16),
            dma((n_tp,)),
            dma((n_tp,)),
            dma((sources,)),
            dma((3,)),
            dma((n_tp - 1, sources)),
            dma((n_tp - 1, sources)),
            dma((CHIPS,)),
            dma((CHIPS,)),
            dma((CHIPS,)),
            dma((CHIPS,)),
            dma((2, streams, 2)),
            dma((2, streams, 2)),
            dma((LAST - 1, streams)),
            dma((LAST - 1, streams)),
            dma((n_tp - 1, 2)),
            dma((n_tp - 1, 2)),
            dma((LAST,)),
            dma((LAST,)),
            dma((LAST,)),
            dma((LAST,)),
        ],
        compiler_params=pltpu.CompilerParams(
            collective_id=0, has_side_effects=True, vmem_limit_bytes=56 * 1024 * 1024
        ),
        name="moe_down_combine",
    )(hidden, down_weight, routes.T, route_weight.T, residual)


def solution(mesh):
    return jax.shard_map(
        on_device,
        mesh=mesh,
        in_specs=(
            P("expert", "dp", None, "tp"),
            P("expert", "tp", None),
            P(("dp", "expert"), None),
            P(("dp", "expert"), None),
            P(("dp", "expert"), "tp"),
        ),
        out_specs=P(("dp", "expert"), "tp"),
        check_vma=False,
    )
```

```python
import jax
import jax.numpy as jnp
from jax import lax
from jax.experimental import pallas as pl
from jax.experimental.pallas import tpu as pltpu
from jax.sharding import PartitionSpec as P

MESH = pl.DeviceIdType.MESH

CHIPS = 8
LAST = CHIPS - 1
SLICE_SHIFT = (3, 1, 2, 0)
HOPS = ((0, 2, 1, 3), (1, 2, 0, 3))
TP_FIRST = 512
STREAM = 256

SETS = ((1, -1), (1, 0), (2, 0), (3, 0), (4, 0), (5, 0), (6, 0), (7, 0), (2, 1), (3, -1), (4, 1))

ORDER = (
    8, 16, 17, 72, 9, 80, 2, 128, 384, 385, 521, 24, 25, 200, 531, 88, 10, 136,
    32, 210, 96, 33, 386, 537, 544, 129, 18, 225, 34, 40, 219, 144, 48, 3, 216, 227,
    137, 387, 11, 112, 160, 218, 41, 226, 26, 104, 145, 450, 560, 152, 553, 35, 232, 19,
    49, 234, 50, 243, 242, 42, 241, 235, 168, 27, 458, 161, 153, 466, 176, 56, 120, 524,
    169, 266, 482, 57, 533, 256, 474, 259, 257, 541, 177, 51, 320, 548, 58, 43, 220, 490,
    229, 184, 498, 557, 321, 564, 236, 185, 245, 322, 59, 506,
)
FIRST_LOADS = ((False, (0, 2)), (True, (0, 1)), (False, (1, 3)), (True, (2, 3)))
ROW_ORDER = [code // 8 for code in ORDER if code < 64 and code % 8 == 0]
WORDS = tuple(
    sum(code << 10 * j for j, code in enumerate(ORDER[t : t + 3])) for t in range(0, len(ORDER), 3)
)


def kernel(
    hidden, weight, routes, scores, residual, out,
    w_early, w_late, h_buf, part, ring_in, blocks, hand_b, hand_a, raw_in, tok, tok_in, late, late_in,
    all_routes, all_scores, rest, counts, table, upright, pick_hi, pick_lo,
    we_sem, wl_sem, h_sem, own_sem, ring_send, ring_recv, hb_send, hb_recv, ha_send, ha_recv, raw_send, raw_recv,
    tok_send, tok_recv, late_send, late_recv, route_send, route_recv, score_send, score_recv,
):
    expert, tp = lax.axis_index("expert"), lax.axis_index("tp")
    n_tp = len(SLICE_SHIFT)
    n_early = TP_FIRST // STREAM
    cap, width = part.shape[2], residual.shape[1]
    tokens = residual.shape[0]
    half = tokens // 2
    f32, bf16 = jnp.float32, jnp.bfloat16
    z, core = expert // 2, lax.rem(expert, 2)
    up, down = lax.rem(tp + 1, n_tp), lax.rem(tp + n_tp - 1, n_tp)
    partner = 2 * z + 1 - core

    def chip(shift):
        return lax.rem(z + shift + CHIPS, CHIPS)

    def ahead(i):
        return (CHIPS // 2 - (i + 1) // 2) * (1 if i % 2 == 1 else -1)

    def w_load(r, early):
        start = lax.rem(tp + SLICE_SHIFT[r], n_tp) * width
        if early:
            at = pl.ds(pl.multiple_of(start, STREAM), TP_FIRST)
            return pltpu.make_async_copy(weight.at[0, :, at], w_early.at[r], we_sem.at[r])
        at = pl.ds(pl.multiple_of(start + TP_FIRST, STREAM), STREAM)
        return pltpu.make_async_copy(
            weight.at[0, :, at], w_late.at[:, pl.ds(r * STREAM, STREAM)], wl_sem.at[r]
        )

    def h_load(i, other):
        source = 2 * chip(ahead(i)) + (1 - core if other else core)
        return pltpu.make_async_copy(hidden.at[0, source], h_buf.at[2 * i + other], h_sem.at[2 * i + other])

    for other in range(2):
        h_load(0, other).start()
    early, rs = FIRST_LOADS[0]
    for r in rs:
        w_load(r, early).start()

    barrier = pltpu.get_barrier_semaphore()
    for peer in (up, down):
        pl.semaphore_signal(barrier, inc=1, device_id={"tp": peer}, device_id_type=MESH)
    greeted = [2 * chip(-ahead(i)) + core for i in range(1, LAST)]
    greeted += [partner, 2 * chip(1) + 1 - core, 2 * chip(-1) + 1 - core]
    for peer in greeted:
        pl.semaphore_signal(barrier, inc=1, device_id={"expert": peer}, device_id_type=MESH)

    for early, rs in FIRST_LOADS[1:]:
        for r in rs:
            w_load(r, early).start()
    for i in ROW_ORDER:
        for other in range(2):
            h_load(i, other).start()

    own_copies = [
        pltpu.make_async_copy(routes, all_routes.at[LAST], own_sem.at[0]),
        pltpu.make_async_copy(scores, all_scores.at[LAST], own_sem.at[1]),
        pltpu.make_async_copy(residual, rest, own_sem.at[2]),
    ]
    for copy in own_copies:
        copy.start()

    def route_copies(i):
        peer = {"expert": 2 * chip(-ahead(i)) + core}
        return [
            pltpu.make_async_remote_copy(
                src_ref=src, dst_ref=dst.at[i], send_sem=send.at[i], recv_sem=recv.at[i],
                device_id=peer, device_id_type=MESH,
            )
            for src, dst, send, recv in (
                (routes, all_routes, route_send, route_recv),
                (scores, all_scores, score_send, score_recv),
            )
        ]

    def ring_part(way, hop):
        first, second = HOPS[way][0], HOPS[way][2]
        return jnp.where(hop == 0, first, jnp.where(hop == 2, second, 2))

    def ring_copy(i, way, hop):
        k = 2 * i + way
        return pltpu.make_async_remote_copy(
            src_ref=part.at[k, ring_part(way, hop)],
            dst_ref=ring_in.at[hop, k],
            send_sem=ring_send.at[hop, k],
            recv_sem=ring_recv.at[hop, k],
            device_id={"tp": (up, down)[way]},
            device_id_type=MESH,
        )

    def late_copy(way, hop):
        return pltpu.make_async_remote_copy(
            src_ref=late.at[ring_part(way, hop), pl.ds(way * half, half)],
            dst_ref=late_in.at[hop, way],
            send_sem=late_send.at[hop, way],
            recv_sem=late_recv.at[hop, way],
            device_id={"tp": (up, down)[way]},
            device_id_type=MESH,
        )

    def hand_copy(i, early):
        first, count = (n_tp, n_early) if early else (0, n_tp)
        source, send, recv = (hand_a, ha_send, ha_recv) if early else (hand_b, hb_send, hb_recv)
        return pltpu.make_async_remote_copy(
            src_ref=source.at[i],
            dst_ref=blocks.at[i, pl.ds(first, count), 1],
            send_sem=send.at[i],
            recv_sem=recv.at[i],
            device_id={"expert": partner},
            device_id_type=MESH,
        )

    def goes_up(s):
        return s in (0, 1, n_tp)

    def raw_from(stage, s):
        return 0 if stage == 0 else 2 if goes_up(s) else 1

    def raw_copy(stage, s, other):
        i = raw_from(stage, s)
        source = (hand_b.at[i, s] if s < n_tp else hand_a.at[i, s - n_tp]) if other else blocks.at[i, s, 0]
        target = chip(1 if goes_up(s) == (stage == 0) else -1)
        return pltpu.make_async_remote_copy(
            src_ref=source,
            dst_ref=raw_in.at[stage, s, other],
            send_sem=raw_send.at[stage, s, other],
            recv_sem=raw_recv.at[stage, s, other],
            device_id={"expert": 2 * target + (1 - core if other else core)},
            device_id_type=MESH,
        )

    def raw_start(i, streams):
        for stage in range(2):
            chosen = [s for s in streams if raw_from(stage, s) == i]
            for s in chosen:
                for other in range(2):
                    raw_copy(stage, s, other).start()

    def raw_wait(stage, s):
        for other in range(2):
            pltpu.make_async_remote_copy(
                src_ref=raw_in.at[stage, s, other], dst_ref=raw_in.at[stage, s, other],
                send_sem=raw_send.at[stage, s, other], recv_sem=raw_recv.at[stage, s, other],
                device_id={"expert": partner}, device_id_type=MESH,
            ).wait_recv()

    def tok_copy(i, s, target):
        return pltpu.make_async_remote_copy(
            src_ref=tok.at[i - 1, s],
            dst_ref=tok_in.at[i - 1, s],
            send_sem=tok_send.at[i - 1, s],
            recv_sem=tok_recv.at[i - 1, s],
            device_id={"expert": 2 * target + core},
            device_id_type=MESH,
        )

    def left_rows(i):
        return h_buf[pl.ds(2 * i, 2)].reshape(2 * cap, h_buf.shape[2])

    def await_rows(i):
        for other in range(2):
            k = 2 * i + other
            pltpu.make_async_copy(hidden.at[0, 0], h_buf.at[k], h_sem.at[k]).wait()

    def product_early(i, r):
        product = jnp.dot(left_rows(i), w_early[r], preferred_element_type=f32)
        part[pl.ds(2 * i, 2), r] = product.astype(bf16).reshape(2, cap, TP_FIRST)

    def matmul_early(i, r):
        for new in (2, 3):
            @pl.when((i == 0) & (r == new))
            def _():
                w_load(new, True).wait()

        @pl.when(r == 0)
        def _():
            await_rows(i)

        product_early(i, r)
        for way in range(2):
            @pl.when(r == way)
            def _():
                ring_copy(i, way, 0).start()

    def product_late(i):
        product = jnp.dot(left_rows(i), w_late[...], preferred_element_type=f32).astype(bf16)
        for r in range(n_tp):
            piece = product[:, r * STREAM : (r + 1) * STREAM]
            blocks[i, r, 0] = piece[:cap]
            hand_b[i, r] = piece[cap:]

    def matmul_late(i, x):
        product_late(i)
        for begin in (1, 2):
            @pl.when(i == begin)
            def _():
                raw_start(begin, range(n_tp))

        hand_copy(i, False).start()

    def arrive(i, hop):
        for way in range(2):
            ring_copy(i, way, hop).wait_recv()
        for way in range(2):
            k, r = 2 * i + way, ring_part(way, hop + 1)
            part[k, r] = part[k, r] + ring_in[hop, k]
        for way in range(2):
            ring_copy(i, way, hop + 1).start()

    def arrive_last(i, x):
        hop = n_tp - 2
        for way in range(2):
            ring_copy(i, way, hop).wait_recv()
        for way in range(2):
            k = 2 * i + way
            for h in range(n_early):
                at = slice(h * STREAM, (h + 1) * STREAM)
                piece = part[k, n_tp - 1, :, at] + ring_in[hop, k, :, at]
                if way == 0:
                    blocks[i, n_tp + h, 0] = piece
                else:
                    hand_a[i, h] = piece

        for begin in range(3):
            @pl.when(i == begin)
            def _():
                raw_start(begin, range(n_tp, n_tp + n_early))

        @pl.when(i > 0)
        def _():
            hand_copy(i, True).start()

    def pick(j, rows):
        return jnp.dot(pick_hi[j], rows, preferred_element_type=f32) + jnp.dot(
            pick_lo[j], rows, preferred_element_type=f32
        )

    def weighted(i, s):
        return pick(i, blocks[i, s].reshape(2 * cap, STREAM))

    def chain(i, s):
        total = weighted(i, s)
        forward = (s < 2) | (s == n_tp)
        raw = (i == jnp.where(forward, 1, 2)) | (i == jnp.where(forward, 4, 3))

        @pl.when(raw)
        def _():
            stage = jnp.where(i > 2, 1, 0)
            raw_wait(stage, s)
            more = pick(jnp.where(i == 1, 0, i + LAST - 1), raw_in[stage, s].reshape(2 * cap, STREAM))
            tok[i - 1, s] = (total + more).astype(bf16)

        @pl.when(jnp.logical_not(raw))
        def _():
            tok_copy(i - 2, s, z).wait_recv()
            tok[i - 1, s] = (total + tok_in[i - 3, s].astype(f32)).astype(bf16)

        tok_copy(i, s, chip(jnp.where(lax.rem(i, 2) == 1, 1, -1))).start()

    def chain_first(i, s):
        @pl.when(s < n_tp)
        def _():
            hand_copy(i, False).wait_recv()

        @pl.when(s >= n_tp)
        def _():
            hand_copy(i, True).wait_recv()

        chain(i, s)

    def chain_end(s, total):
        for i in (LAST - 2, LAST - 1):
            tok_copy(i, s, z).wait_recv()
        return total + tok_in[LAST - 3, s].astype(f32) + tok_in[LAST - 2, s].astype(f32)

    def end_late(first, s):
        @pl.when(first == 1)
        def _():
            hand_copy(LAST, False).wait_recv()

        late[s] = chain_end(s, weighted(LAST, s)).astype(bf16)

    def late_step(i, x):
        @pl.when(x > 0)
        def _():
            for way in range(2):
                late_copy(way, x - 1).wait_recv()
            for way in range(2):
                here = pl.ds(way * half, half)
                r = ring_part(way, x)
                late[r, here] = late[r, here] + late_in[x - 1, way]

        for way in range(2):
            late_copy(way, x).start()

    def selection_table():
        rows = lax.broadcasted_iota(jnp.int32, (tokens, tokens), 0)
        cols = lax.broadcasted_iota(jnp.int32, (tokens, tokens), 1)
        earlier = jnp.where(rows < cols, 1.0, 0.0).astype(bf16)
        for j in range(1, LAST):
            for copy in route_copies(j):
                copy.wait_recv()
        for copy in own_copies[:2]:
            copy.wait()
        for j, (group, shift) in enumerate(SETS):
            chosen, value = all_routes[group], all_scores[group]
            share = value / jnp.sum(value, axis=0, keepdims=True)
            for q in range(2):
                same = chosen == 2 * chip(shift) + (1 - core if q else core)
                line = 2 * j + q
                counts[line : line + 1, :] = jnp.sum(jnp.where(same, 1.0, 0.0), axis=0, keepdims=True)
                table[96 + line : 97 + line, :] = jnp.sum(jnp.where(same, share, 0.0), axis=0, keepdims=True)
        used = 2 * len(SETS)
        counts[used:, :] = jnp.zeros((counts.shape[0] - used, tokens), f32)
        table[96 + used :, :] = jnp.zeros((32 - used, tokens), f32)
        member = counts[...]
        before = jnp.dot(member.astype(bf16), earlier, preferred_element_type=f32)
        second = lax.rem(lax.broadcasted_iota(jnp.int32, member.shape, 0), 2) == 1
        portion = table[96:128, :]
        portion_hi = portion.astype(bf16).astype(f32)
        table[0:32, :] = jnp.where(member > 0.5, before + jnp.where(second, float(cap), 0.0), -1.0)
        table[32:64, :] = portion_hi
        table[64:96, :] = portion - portion_hi
        upright[...] = jnp.transpose(table[...])

    def selection_sets(sets):
        column = lax.broadcasted_iota(jnp.int32, (tokens, 2 * cap), 1).astype(f32)
        for j in sets:
            own, other = (column == upright[:, 2 * j + q : 2 * j + q + 1] for q in range(2))
            for target, base in ((pick_hi, 32), (pick_lo, 64)):
                a, b = (upright[:, base + 2 * j + q : base + 2 * j + q + 1] for q in range(2))
                target[j] = jnp.where(own, a, jnp.where(other, b, 0.0)).astype(bf16)

    def selection(i, x):
        pl.when(x == 0)(selection_table)
        for stage, sets in enumerate(((0, 8, 1, 2), (3, 4, 9, 10), (5, 6, 7))):
            @pl.when(x == stage + 1)
            def _():
                selection_sets(sets)

    def nothing(i, x):
        pass

    kinds = (
        matmul_early, matmul_late, arrive, chain, end_late, late_step, selection, arrive_last, chain_first,
        nothing,
    )

    def first_late(r):
        w_load(r, False).wait()
        at = slice(r * STREAM, (r + 1) * STREAM)
        product = jnp.dot(left_rows(0), w_late[:, at], preferred_element_type=f32).astype(bf16)
        blocks[0, r, 0] = product[:cap]
        hand_b[0, r] = product[cap:]

    await_rows(0)
    first_late(0)
    pl.semaphore_wait(barrier, 2 + len(greeted))
    for i in range(1, LAST):
        for copy in route_copies(i):
            copy.start()
    raw_start(0, (0,))
    first_late(2)
    raw_start(0, (2,))
    for way in range(2):
        w_load(way, True).wait()
        product_early(0, way)
        ring_copy(0, way, 0).start()
    for r in (1, 3):
        first_late(r)
        raw_start(0, (r,))

    def steps(j, carry):
        word = jnp.int32(WORDS[0])
        for n in range(1, len(WORDS)):
            word = jnp.where(j == n, WORDS[n], word)

        def step(m, inner):
            code = lax.rem(lax.shift_right_logical(word, 10 * m), 1024)
            i, x = lax.rem(code // 8, 8), lax.rem(code, 8)

            def branch(kind):
                def run():
                    kind(i, x)

                return run

            lax.switch(code // 64, [branch(kind) for kind in kinds])
            return inner

        lax.fori_loop(0, 3, step, 0)
        return carry

    lax.fori_loop(0, len(WORDS), steps, 0)

    own_copies[2].wait()
    for way in range(2):
        late_copy(way, n_tp - 2).wait_recv()
        here = slice(way * half, (way + 1) * half)
        mixed = late[n_tp - 1, here].astype(f32) + late_in[n_tp - 2, way].astype(f32)
        out[here, TP_FIRST:] = (rest[here, TP_FIRST:].astype(f32) + mixed).astype(bf16)
    hand_copy(LAST, True).wait_recv()
    totals = []
    for h in range(n_early):
        at = slice(h * STREAM, (h + 1) * STREAM)
        totals.append(rest[:, at].astype(f32) + weighted(LAST, n_tp + h))
    for h in range(n_early):
        out[:, h * STREAM : (h + 1) * STREAM] = chain_end(n_tp + h, totals[h]).astype(bf16)

    def drain(i, carry):
        for hop in range(n_tp - 1):
            for way in range(2):
                ring_copy(i, way, hop).wait_send()

        @pl.when(i > 0)
        def _():
            for early in (False, True):
                hand_copy(i, early).wait_send()

        @pl.when((i > 0) & (i < LAST))
        def _():
            for s in range(blocks.shape[1]):
                @pl.when(i != (2 if goes_up(s) else 1))
                def _():
                    tok_copy(i, s, z).wait_send()

        return carry

    lax.fori_loop(0, CHIPS, drain, 0)
    for stage in range(2):
        for s in range(blocks.shape[1]):
            for other in range(2):
                raw_copy(stage, s, other).wait_send()
    for i in range(1, LAST):
        for copy in route_copies(i):
            copy.wait_send()
    for hop in range(n_tp - 1):
        for way in range(2):
            late_copy(way, hop).wait_send()


def on_device(hidden, down_weight, routes, route_weight, residual):
    sources, cap, units = hidden.shape[1:]
    tokens, width = residual.shape
    top = routes.shape[1]
    n_tp = len(SLICE_SHIFT)
    early = TP_FIRST // STREAM
    streams = n_tp + early
    bf16, f32 = jnp.bfloat16, jnp.float32
    any_space = pl.BlockSpec(memory_space=pl.ANY)
    dma = pltpu.SemaphoreType.DMA
    return pl.pallas_call(
        kernel,
        out_shape=pltpu.VMEM((tokens, width), bf16),
        in_specs=[any_space] * 5,
        out_specs=pl.BlockSpec(memory_space=pltpu.VMEM),
        scratch_shapes=[
            pltpu.VMEM((n_tp, units, TP_FIRST), bf16),
            pltpu.VMEM((units, n_tp * STREAM), bf16),
            pltpu.VMEM((sources, cap, units), bf16),
            pltpu.VMEM((sources, n_tp, cap, TP_FIRST), bf16),
            pltpu.VMEM((n_tp - 1, sources, cap, TP_FIRST), bf16),
            pltpu.VMEM((CHIPS, streams, 2, cap, STREAM), bf16),
            pltpu.VMEM((CHIPS, n_tp, cap, STREAM), bf16),
            pltpu.VMEM((CHIPS, early, cap, STREAM), bf16),
            pltpu.VMEM((2, streams, 2, cap, STREAM), bf16),
            pltpu.VMEM((LAST - 1, streams, tokens, STREAM), bf16),
            pltpu.VMEM((LAST - 1, streams, tokens, STREAM), bf16),
            pltpu.VMEM((n_tp, tokens, STREAM), bf16),
            pltpu.VMEM((n_tp - 1, 2, tokens // 2, STREAM), bf16),
            pltpu.VMEM((CHIPS, top, tokens), jnp.int32),
            pltpu.VMEM((CHIPS, top, tokens), f32),
            pltpu.VMEM((tokens, width), bf16),
            pltpu.VMEM((32, tokens), f32),
            pltpu.VMEM((128, tokens), f32),
            pltpu.VMEM((tokens, 128), f32),
            pltpu.VMEM((len(SETS), tokens, 2 * cap), bf16),
            pltpu.VMEM((len(SETS), tokens, 2 * cap), bf16),
            dma((n_tp,)),
            dma((n_tp,)),
            dma((sources,)),
            dma((3,)),
            dma((n_tp - 1, sources)),
            dma((n_tp - 1, sources)),
            dma((CHIPS,)),
            dma((CHIPS,)),
            dma((CHIPS,)),
            dma((CHIPS,)),
            dma((2, streams, 2)),
            dma((2, streams, 2)),
            dma((LAST - 1, streams)),
            dma((LAST - 1, streams)),
            dma((n_tp - 1, 2)),
            dma((n_tp - 1, 2)),
            dma((LAST,)),
            dma((LAST,)),
            dma((LAST,)),
            dma((LAST,)),
        ],
        compiler_params=pltpu.CompilerParams(
            collective_id=0, has_side_effects=True, vmem_limit_bytes=56 * 1024 * 1024
        ),
        name="moe_down_combine",
    )(hidden, down_weight, routes.T, route_weight.T, residual)


def solution(mesh):
    return jax.shard_map(
        on_device,
        mesh=mesh,
        in_specs=(
            P("expert", "dp", None, "tp"),
            P("expert", "tp", None),
            P(("dp", "expert"), None),
            P(("dp", "expert"), None),
            P(("dp", "expert"), "tp"),
        ),
        out_specs=P(("dp", "expert"), "tp"),
        check_vma=False,
    )
```

```python
import jax
import jax.numpy as jnp
from jax import lax
from jax.experimental import pallas as pl
from jax.experimental.pallas import tpu as pltpu
from jax.sharding import PartitionSpec as P

MESH = pl.DeviceIdType.MESH

CHIPS = 8
LAST = CHIPS - 1
SLICE_SHIFT = (3, 1, 2, 0)
HOPS = ((0, 2, 1, 3), (1, 2, 0, 3))
TP_FIRST = 512
STREAM = 256

SETS = ((1, -1), (1, 0), (2, 0), (3, 0), (4, 0), (5, 0), (6, 0), (7, 0), (2, 1), (3, -1), (4, 1))

ORDER = (
    8, 16, 17, 72, 9, 80, 2, 128, 384, 385, 521, 24, 25, 200, 531, 88, 10, 136,
    32, 210, 96, 33, 386, 537, 544, 129, 18, 225, 34, 40, 219, 144, 48, 3, 216, 227,
    137, 387, 11, 112, 160, 218, 41, 226, 26, 104, 145, 450, 560, 152, 553, 35, 232, 19,
    49, 234, 50, 243, 242, 42, 241, 235, 168, 27, 458, 161, 153, 466, 176, 56, 120, 524,
    169, 266, 482, 57, 533, 256, 474, 259, 257, 541, 177, 51, 320, 548, 58, 43, 220, 490,
    229, 184, 498, 557, 321, 564, 236, 185, 245, 322, 59, 506,
)
FIRST_LOADS = ((False, (0, 2)), (True, (0, 1)), (False, (1, 3)), (True, (2, 3)))
ROW_ORDER = [code // 8 for code in ORDER if code < 64 and code % 8 == 0]
WORDS = tuple(
    sum(code << 10 * j for j, code in enumerate(ORDER[t : t + 3])) for t in range(0, len(ORDER), 3)
)


def kernel(
    hidden, weight, routes, scores, residual, out,
    w_early, w_late, h_buf, part, ring_in, blocks, hand_b, hand_a, raw_in, tok, tok_in, late, late_in,
    all_routes, all_scores, rest, counts, table, upright, pick_hi, pick_lo,
    we_sem, wl_sem, h_sem, own_sem, ring_send, ring_recv, hb_send, hb_recv, ha_send, ha_recv, raw_send, raw_recv,
    tok_send, tok_recv, late_send, late_recv, route_send, route_recv, score_send, score_recv,
):
    expert, tp = lax.axis_index("expert"), lax.axis_index("tp")
    n_tp = len(SLICE_SHIFT)
    n_early = TP_FIRST // STREAM
    cap, width = part.shape[2], residual.shape[1]
    tokens = residual.shape[0]
    half = tokens // 2
    f32, bf16 = jnp.float32, jnp.bfloat16
    z, core = expert // 2, lax.rem(expert, 2)
    up, down = lax.rem(tp + 1, n_tp), lax.rem(tp + n_tp - 1, n_tp)
    partner = 2 * z + 1 - core

    def chip(shift):
        return lax.rem(z + shift + CHIPS, CHIPS)

    def ahead(i):
        return (CHIPS // 2 - (i + 1) // 2) * (1 if i % 2 == 1 else -1)

    def w_load(r, early):
        start = lax.rem(tp + SLICE_SHIFT[r], n_tp) * width
        if early:
            at = pl.ds(pl.multiple_of(start, STREAM), TP_FIRST)
            return pltpu.make_async_copy(weight.at[0, :, at], w_early.at[r], we_sem.at[r])
        at = pl.ds(pl.multiple_of(start + TP_FIRST, STREAM), STREAM)
        return pltpu.make_async_copy(
            weight.at[0, :, at], w_late.at[:, pl.ds(r * STREAM, STREAM)], wl_sem.at[r]
        )

    def h_load(i, other):
        source = 2 * chip(ahead(i)) + (1 - core if other else core)
        return pltpu.make_async_copy(hidden.at[0, source], h_buf.at[2 * i + other], h_sem.at[2 * i + other])

    for other in range(2):
        h_load(0, other).start()
    early, rs = FIRST_LOADS[0]
    for r in rs:
        w_load(r, early).start()

    barrier = pltpu.get_barrier_semaphore()
    for peer in (up, down):
        pl.semaphore_signal(barrier, inc=1, device_id={"tp": peer}, device_id_type=MESH)
    greeted = [2 * chip(-ahead(i)) + core for i in range(1, LAST)]
    greeted += [partner, 2 * chip(1) + 1 - core, 2 * chip(-1) + 1 - core]
    for peer in greeted:
        pl.semaphore_signal(barrier, inc=1, device_id={"expert": peer}, device_id_type=MESH)

    for early, rs in FIRST_LOADS[1:]:
        for r in rs:
            w_load(r, early).start()
    for i in ROW_ORDER:
        for other in range(2):
            h_load(i, other).start()

    own_copies = [
        pltpu.make_async_copy(routes, all_routes.at[LAST], own_sem.at[0]),
        pltpu.make_async_copy(scores, all_scores.at[LAST], own_sem.at[1]),
        pltpu.make_async_copy(residual, rest, own_sem.at[2]),
    ]
    for copy in own_copies:
        copy.start()

    def route_copies(i):
        peer = {"expert": 2 * chip(-ahead(i)) + core}
        return [
            pltpu.make_async_remote_copy(
                src_ref=src, dst_ref=dst.at[i], send_sem=send.at[i], recv_sem=recv.at[i],
                device_id=peer, device_id_type=MESH,
            )
            for src, dst, send, recv in (
                (routes, all_routes, route_send, route_recv),
                (scores, all_scores, score_send, score_recv),
            )
        ]

    def ring_part(way, hop):
        first, second = HOPS[way][0], HOPS[way][2]
        return jnp.where(hop == 0, first, jnp.where(hop == 2, second, 2))

    def ring_copy(i, way, hop):
        k = 2 * i + way
        return pltpu.make_async_remote_copy(
            src_ref=part.at[k, ring_part(way, hop)],
            dst_ref=ring_in.at[hop, k],
            send_sem=ring_send.at[hop, k],
            recv_sem=ring_recv.at[hop, k],
            device_id={"tp": (up, down)[way]},
            device_id_type=MESH,
        )

    def late_copy(way, hop):
        return pltpu.make_async_remote_copy(
            src_ref=late.at[ring_part(way, hop), pl.ds(way * half, half)],
            dst_ref=late_in.at[hop, way],
            send_sem=late_send.at[hop, way],
            recv_sem=late_recv.at[hop, way],
            device_id={"tp": (up, down)[way]},
            device_id_type=MESH,
        )

    def hand_copy(i, early):
        first, count = (n_tp, n_early) if early else (0, n_tp)
        source, send, recv = (hand_a, ha_send, ha_recv) if early else (hand_b, hb_send, hb_recv)
        return pltpu.make_async_remote_copy(
            src_ref=source.at[i],
            dst_ref=blocks.at[i, pl.ds(first, count), 1],
            send_sem=send.at[i],
            recv_sem=recv.at[i],
            device_id={"expert": partner},
            device_id_type=MESH,
        )

    def goes_up(s):
        return s in (0, 1, n_tp)

    def raw_from(stage, s):
        return 0 if stage == 0 else 2 if goes_up(s) else 1

    def raw_copy(stage, s, other):
        i = raw_from(stage, s)
        source = (hand_b.at[i, s] if s < n_tp else hand_a.at[i, s - n_tp]) if other else blocks.at[i, s, 0]
        target = chip(1 if goes_up(s) == (stage == 0) else -1)
        return pltpu.make_async_remote_copy(
            src_ref=source,
            dst_ref=raw_in.at[stage, s, other],
            send_sem=raw_send.at[stage, s, other],
            recv_sem=raw_recv.at[stage, s, other],
            device_id={"expert": 2 * target + (1 - core if other else core)},
            device_id_type=MESH,
        )

    def raw_start(i, streams):
        for stage in range(2):
            chosen = [s for s in streams if raw_from(stage, s) == i]
            for s in chosen:
                for other in range(2):
                    raw_copy(stage, s, other).start()

    def raw_wait(stage, s):
        for other in range(2):
            pltpu.make_async_remote_copy(
                src_ref=raw_in.at[stage, s, other], dst_ref=raw_in.at[stage, s, other],
                send_sem=raw_send.at[stage, s, other], recv_sem=raw_recv.at[stage, s, other],
                device_id={"expert": partner}, device_id_type=MESH,
            ).wait_recv()

    def tok_copy(i, s, target):
        return pltpu.make_async_remote_copy(
            src_ref=tok.at[i - 1, s],
            dst_ref=tok_in.at[i - 1, s],
            send_sem=tok_send.at[i - 1, s],
            recv_sem=tok_recv.at[i - 1, s],
            device_id={"expert": 2 * target + core},
            device_id_type=MESH,
        )

    def left_rows(i):
        return h_buf[pl.ds(2 * i, 2)].reshape(2 * cap, h_buf.shape[2])

    def await_rows(i):
        for other in range(2):
            k = 2 * i + other
            pltpu.make_async_copy(hidden.at[0, 0], h_buf.at[k], h_sem.at[k]).wait()

    def product_early(i, r):
        product = jnp.dot(left_rows(i), w_early[r], preferred_element_type=f32)
        part[pl.ds(2 * i, 2), r] = product.astype(bf16).reshape(2, cap, TP_FIRST)

    def matmul_early(i, r):
        for new in (2, 3):
            @pl.when((i == 0) & (r == new))
            def _():
                w_load(new, True).wait()

        @pl.when(r == 0)
        def _():
            await_rows(i)

        product_early(i, r)
        for way in range(2):
            @pl.when(r == way)
            def _():
                ring_copy(i, way, 0).start()

    def product_late(i):
        product = jnp.dot(left_rows(i), w_late[...], preferred_element_type=f32).astype(bf16)
        for r in range(n_tp):
            piece = product[:, r * STREAM : (r + 1) * STREAM]
            blocks[i, r, 0] = piece[:cap]
            hand_b[i, r] = piece[cap:]

    def matmul_late(i, x):
        product_late(i)
        for begin in (1, 2):
            @pl.when(i == begin)
            def _():
                raw_start(begin, range(n_tp))

        hand_copy(i, False).start()

    def arrive(i, hop):
        for way in range(2):
            ring_copy(i, way, hop).wait_recv()
        for way in range(2):
            k, r = 2 * i + way, ring_part(way, hop + 1)
            part[k, r] = part[k, r] + ring_in[hop, k]
        for way in range(2):
            ring_copy(i, way, hop + 1).start()

    def arrive_last(i, x):
        hop = n_tp - 2
        for way in range(2):
            ring_copy(i, way, hop).wait_recv()
        for way in range(2):
            k = 2 * i + way
            for h in range(n_early):
                at = slice(h * STREAM, (h + 1) * STREAM)
                piece = part[k, n_tp - 1, :, at] + ring_in[hop, k, :, at]
                if way == 0:
                    blocks[i, n_tp + h, 0] = piece
                else:
                    hand_a[i, h] = piece

        for begin in range(3):
            @pl.when(i == begin)
            def _():
                raw_start(begin, range(n_tp, n_tp + n_early))

        @pl.when(i > 0)
        def _():
            hand_copy(i, True).start()

    def pick(j, rows):
        return jnp.dot(pick_hi[j], rows, preferred_element_type=f32) + jnp.dot(
            pick_lo[j], rows, preferred_element_type=f32
        )

    def weighted(i, s):
        return pick(i, blocks[i, s].reshape(2 * cap, STREAM))

    def chain(i, s):
        total = weighted(i, s)
        forward = (s < 2) | (s == n_tp)
        raw = (i == jnp.where(forward, 1, 2)) | (i == jnp.where(forward, 4, 3))

        @pl.when(raw)
        def _():
            stage = jnp.where(i > 2, 1, 0)
            raw_wait(stage, s)
            more = pick(jnp.where(i == 1, 0, i + LAST - 1), raw_in[stage, s].reshape(2 * cap, STREAM))
            tok[i - 1, s] = (total + more).astype(bf16)

        @pl.when(jnp.logical_not(raw))
        def _():
            tok_copy(i - 2, s, z).wait_recv()
            tok[i - 1, s] = (total + tok_in[i - 3, s].astype(f32)).astype(bf16)

        tok_copy(i, s, chip(jnp.where(lax.rem(i, 2) == 1, 1, -1))).start()

    def chain_first(i, s):
        @pl.when(s < n_tp)
        def _():
            hand_copy(i, False).wait_recv()

        @pl.when(s >= n_tp)
        def _():
            hand_copy(i, True).wait_recv()

        chain(i, s)

    def chain_end(s, total):
        for i in (LAST - 2, LAST - 1):
            tok_copy(i, s, z).wait_recv()
        return total + tok_in[LAST - 3, s].astype(f32) + tok_in[LAST - 2, s].astype(f32)

    def end_late(first, s):
        @pl.when(first == 1)
        def _():
            hand_copy(LAST, False).wait_recv()

        late[s] = chain_end(s, weighted(LAST, s)).astype(bf16)

    def late_step(i, x):
        @pl.when(x > 0)
        def _():
            for way in range(2):
                late_copy(way, x - 1).wait_recv()
            for way in range(2):
                here = pl.ds(way * half, half)
                r = ring_part(way, x)
                late[r, here] = late[r, here] + late_in[x - 1, way]

        for way in range(2):
            late_copy(way, x).start()

    def selection_table():
        rows = lax.broadcasted_iota(jnp.int32, (tokens, tokens), 0)
        cols = lax.broadcasted_iota(jnp.int32, (tokens, tokens), 1)
        earlier = jnp.where(rows < cols, 1.0, 0.0).astype(bf16)
        for j in range(1, LAST):
            for copy in route_copies(j):
                copy.wait_recv()
        for copy in own_copies[:2]:
            copy.wait()
        for j, (group, shift) in enumerate(SETS):
            chosen, value = all_routes[group], all_scores[group]
            share = value / jnp.sum(value, axis=0, keepdims=True)
            for q in range(2):
                same = chosen == 2 * chip(shift) + (1 - core if q else core)
                line = 2 * j + q
                counts[line : line + 1, :] = jnp.sum(jnp.where(same, 1.0, 0.0), axis=0, keepdims=True)
                table[96 + line : 97 + line, :] = jnp.sum(jnp.where(same, share, 0.0), axis=0, keepdims=True)
        used = 2 * len(SETS)
        counts[used:, :] = jnp.zeros((counts.shape[0] - used, tokens), f32)
        table[96 + used :, :] = jnp.zeros((32 - used, tokens), f32)
        member = counts[...]
        before = jnp.dot(member.astype(bf16), earlier, preferred_element_type=f32)
        second = lax.rem(lax.broadcasted_iota(jnp.int32, member.shape, 0), 2) == 1
        portion = table[96:128, :]
        portion_hi = portion.astype(bf16).astype(f32)
        table[0:32, :] = jnp.where(member > 0.5, before + jnp.where(second, float(cap), 0.0), -1.0)
        table[32:64, :] = portion_hi
        table[64:96, :] = portion - portion_hi
        upright[...] = jnp.transpose(table[...])

    def selection_sets(sets):
        column = lax.broadcasted_iota(jnp.int32, (tokens, 2 * cap), 1).astype(f32)
        for j in sets:
            own, other = (column == upright[:, 2 * j + q : 2 * j + q + 1] for q in range(2))
            for target, base in ((pick_hi, 32), (pick_lo, 64)):
                a, b = (upright[:, base + 2 * j + q : base + 2 * j + q + 1] for q in range(2))
                target[j] = jnp.where(own, a, jnp.where(other, b, 0.0)).astype(bf16)

    def selection(i, x):
        pl.when(x == 0)(selection_table)
        for stage, sets in enumerate(((0, 8, 1, 2), (3, 4, 9, 10), (5, 6, 7))):
            @pl.when(x == stage + 1)
            def _():
                selection_sets(sets)

    def nothing(i, x):
        pass

    kinds = (
        matmul_early, matmul_late, arrive, chain, end_late, late_step, selection, arrive_last, chain_first,
        nothing,
    )

    def first_late(r):
        w_load(r, False).wait()
        at = slice(r * STREAM, (r + 1) * STREAM)
        product = jnp.dot(left_rows(0), w_late[:, at], preferred_element_type=f32).astype(bf16)
        blocks[0, r, 0] = product[:cap]
        hand_b[0, r] = product[cap:]

    await_rows(0)
    first_late(0)
    pl.semaphore_wait(barrier, 2 + len(greeted))
    for i in range(1, LAST):
        for copy in route_copies(i):
            copy.start()
    raw_start(0, (0,))
    first_late(2)
    raw_start(0, (2,))
    for way in range(2):
        w_load(way, True).wait()
        product_early(0, way)
        ring_copy(0, way, 0).start()
    for r in (1, 3):
        first_late(r)
        raw_start(0, (r,))

    def steps(j, carry):
        word = jnp.int32(WORDS[0])
        for n in range(1, len(WORDS)):
            word = jnp.where(j == n, WORDS[n], word)

        def step(m, inner):
            code = lax.rem(lax.shift_right_logical(word, 10 * m), 1024)
            i, x = lax.rem(code // 8, 8), lax.rem(code, 8)

            def branch(kind):
                def run():
                    kind(i, x)

                return run

            lax.switch(code // 64, [branch(kind) for kind in kinds])
            return inner

        lax.fori_loop(0, 3, step, 0)
        return carry

    lax.fori_loop(0, len(WORDS), steps, 0)

    def settle_blocks(i, carry):
        for hop in range(n_tp - 1):
            for way in range(2):
                ring_copy(i, way, hop).wait_send()

        @pl.when(i > 0)
        def _():
            for early in (False, True):
                hand_copy(i, early).wait_send()

        return carry

    def settle_sums(i, carry):
        for s in range(blocks.shape[1]):
            @pl.when(i != (2 if goes_up(s) else 1))
            def _():
                tok_copy(i, s, z).wait_send()

        return carry

    lax.fori_loop(0, LAST, settle_blocks, 0)
    lax.fori_loop(1, LAST - 2, settle_sums, 0)
    for stage in range(2):
        for s in range(blocks.shape[1]):
            for other in range(2):
                raw_copy(stage, s, other).wait_send()
    for i in range(1, LAST):
        for copy in route_copies(i):
            copy.wait_send()
    for hop in range(n_tp - 2):
        for way in range(2):
            late_copy(way, hop).wait_send()

    own_copies[2].wait()
    for way in range(2):
        late_copy(way, n_tp - 2).wait_recv()
        here = slice(way * half, (way + 1) * half)
        mixed = late[n_tp - 1, here].astype(f32) + late_in[n_tp - 2, way].astype(f32)
        out[here, TP_FIRST:] = (rest[here, TP_FIRST:].astype(f32) + mixed).astype(bf16)
    hand_copy(LAST, True).wait_recv()
    totals = []
    for h in range(n_early):
        at = slice(h * STREAM, (h + 1) * STREAM)
        totals.append(rest[:, at].astype(f32) + weighted(LAST, n_tp + h))
    for h in range(n_early):
        out[:, h * STREAM : (h + 1) * STREAM] = chain_end(n_tp + h, totals[h]).astype(bf16)

    for s in range(blocks.shape[1]):
        for i in (LAST - 2, LAST - 1):
            tok_copy(i, s, z).wait_send()
    settle_blocks(jnp.int32(LAST), 0)
    for way in range(2):
        late_copy(way, n_tp - 2).wait_send()


def on_device(hidden, down_weight, routes, route_weight, residual):
    sources, cap, units = hidden.shape[1:]
    tokens, width = residual.shape
    top = routes.shape[1]
    n_tp = len(SLICE_SHIFT)
    early = TP_FIRST // STREAM
    streams = n_tp + early
    bf16, f32 = jnp.bfloat16, jnp.float32
    any_space = pl.BlockSpec(memory_space=pl.ANY)
    dma = pltpu.SemaphoreType.DMA
    return pl.pallas_call(
        kernel,
        out_shape=pltpu.VMEM((tokens, width), bf16),
        in_specs=[any_space] * 5,
        out_specs=pl.BlockSpec(memory_space=pltpu.VMEM),
        scratch_shapes=[
            pltpu.VMEM((n_tp, units, TP_FIRST), bf16),
            pltpu.VMEM((units, n_tp * STREAM), bf16),
            pltpu.VMEM((sources, cap, units), bf16),
            pltpu.VMEM((sources, n_tp, cap, TP_FIRST), bf16),
            pltpu.VMEM((n_tp - 1, sources, cap, TP_FIRST), bf16),
            pltpu.VMEM((CHIPS, streams, 2, cap, STREAM), bf16),
            pltpu.VMEM((CHIPS, n_tp, cap, STREAM), bf16),
            pltpu.VMEM((CHIPS, early, cap, STREAM), bf16),
            pltpu.VMEM((2, streams, 2, cap, STREAM), bf16),
            pltpu.VMEM((LAST - 1, streams, tokens, STREAM), bf16),
            pltpu.VMEM((LAST - 1, streams, tokens, STREAM), bf16),
            pltpu.VMEM((n_tp, tokens, STREAM), bf16),
            pltpu.VMEM((n_tp - 1, 2, tokens // 2, STREAM), bf16),
            pltpu.VMEM((CHIPS, top, tokens), jnp.int32),
            pltpu.VMEM((CHIPS, top, tokens), f32),
            pltpu.VMEM((tokens, width), bf16),
            pltpu.VMEM((32, tokens), f32),
            pltpu.VMEM((128, tokens), f32),
            pltpu.VMEM((tokens, 128), f32),
            pltpu.VMEM((len(SETS), tokens, 2 * cap), bf16),
            pltpu.VMEM((len(SETS), tokens, 2 * cap), bf16),
            dma((n_tp,)),
            dma((n_tp,)),
            dma((sources,)),
            dma((3,)),
            dma((n_tp - 1, sources)),
            dma((n_tp - 1, sources)),
            dma((CHIPS,)),
            dma((CHIPS,)),
            dma((CHIPS,)),
            dma((CHIPS,)),
            dma((2, streams, 2)),
            dma((2, streams, 2)),
            dma((LAST - 1, streams)),
            dma((LAST - 1, streams)),
            dma((n_tp - 1, 2)),
            dma((n_tp - 1, 2)),
            dma((LAST,)),
            dma((LAST,)),
            dma((LAST,)),
            dma((LAST,)),
        ],
        compiler_params=pltpu.CompilerParams(
            collective_id=0, has_side_effects=True, vmem_limit_bytes=56 * 1024 * 1024
        ),
        name="moe_down_combine",
    )(hidden, down_weight, routes.T, route_weight.T, residual)


def solution(mesh):
    return jax.shard_map(
        on_device,
        mesh=mesh,
        in_specs=(
            P("expert", "dp", None, "tp"),
            P("expert", "tp", None),
            P(("dp", "expert"), None),
            P(("dp", "expert"), None),
            P(("dp", "expert"), "tp"),
        ),
        out_specs=P(("dp", "expert"), "tp"),
        check_vma=False,
    )
```

```python
import jax
import jax.numpy as jnp
from jax import lax
from jax.experimental import pallas as pl
from jax.experimental.pallas import tpu as pltpu
from jax.sharding import PartitionSpec as P

MESH = pl.DeviceIdType.MESH

CHIPS = 8
LAST = CHIPS - 1
SLICE_SHIFT = (3, 1, 2, 0)
HOPS = ((0, 2, 1, 3), (1, 2, 0, 3))
TP_FIRST = 512
STREAM = 256

SETS = ((1, -1), (1, 0), (2, 0), (3, 0), (4, 0), (5, 0), (6, 0), (7, 0), (2, 1), (3, -1), (4, 1))

ORDER = (
    8, 16, 17, 72, 9, 80, 2, 128, 384, 385, 521, 24, 25, 200, 531, 88, 10, 136,
    32, 210, 96, 33, 386, 537, 544, 129, 18, 225, 34, 40, 219, 144, 48, 3, 216, 227,
    137, 387, 11, 112, 160, 218, 41, 226, 26, 104, 145, 450, 560, 152, 553, 35, 232, 19,
    49, 234, 50, 243, 242, 42, 241, 235, 168, 27, 458, 161, 153, 466, 176, 56, 120, 524,
    169, 266, 482, 57, 533, 256, 474, 259, 257, 541, 177, 51, 320, 548, 58, 43, 220, 490,
    229, 184, 498, 557, 321, 564, 236, 185, 245, 322, 59, 506,
)
FIRST_LOADS = ((False, (0, 2)), (True, (0, 1)), (False, (1, 3)), (True, (2, 3)))
ROW_ORDER = [code // 8 for code in ORDER if code < 64 and code % 8 == 0]
WORDS = tuple(
    sum(code << 10 * j for j, code in enumerate(ORDER[t : t + 3])) for t in range(0, len(ORDER), 3)
)


def kernel(
    hidden, weight, routes, scores, residual, out,
    w_early, w_late, h_buf, part, ring_in, blocks, hand_b, hand_a, raw_in, tok, tok_in, late, late_in,
    all_routes, all_scores, rest, counts, table, upright, pick_hi, pick_lo,
    we_sem, wl_sem, h_sem, own_sem, ring_send, ring_recv, hb_send, hb_recv, ha_send, ha_recv, raw_send, raw_recv,
    tok_send, tok_recv, late_send, late_recv, route_send, route_recv, score_send, score_recv,
):
    expert, tp = lax.axis_index("expert"), lax.axis_index("tp")
    n_tp = len(SLICE_SHIFT)
    n_early = TP_FIRST // STREAM
    cap, width = part.shape[2], residual.shape[1]
    tokens = residual.shape[0]
    half = tokens // 2
    f32, bf16 = jnp.float32, jnp.bfloat16
    z, core = expert // 2, lax.rem(expert, 2)
    up, down = lax.rem(tp + 1, n_tp), lax.rem(tp + n_tp - 1, n_tp)
    partner = 2 * z + 1 - core

    def chip(shift):
        return lax.rem(z + shift + CHIPS, CHIPS)

    def ahead(i):
        return (CHIPS // 2 - (i + 1) // 2) * (1 if i % 2 == 1 else -1)

    def w_load(r, early):
        start = lax.rem(tp + SLICE_SHIFT[r], n_tp) * width
        if early:
            at = pl.ds(pl.multiple_of(start, STREAM), TP_FIRST)
            return pltpu.make_async_copy(weight.at[0, :, at], w_early.at[r], we_sem.at[r])
        at = pl.ds(pl.multiple_of(start + TP_FIRST, STREAM), STREAM)
        return pltpu.make_async_copy(
            weight.at[0, :, at], w_late.at[:, pl.ds(r * STREAM, STREAM)], wl_sem.at[r]
        )

    def h_load(i, other):
        source = 2 * chip(ahead(i)) + (1 - core if other else core)
        return pltpu.make_async_copy(hidden.at[0, source], h_buf.at[2 * i + other], h_sem.at[2 * i + other])

    for other in range(2):
        h_load(0, other).start()
    early, rs = FIRST_LOADS[0]
    for r in rs:
        w_load(r, early).start()

    barrier = pltpu.get_barrier_semaphore()
    for peer in (up, down):
        pl.semaphore_signal(barrier, inc=1, device_id={"tp": peer}, device_id_type=MESH)
    greeted = [2 * chip(-ahead(i)) + core for i in range(1, LAST)]
    greeted += [partner, 2 * chip(1) + 1 - core, 2 * chip(-1) + 1 - core]
    for peer in greeted:
        pl.semaphore_signal(barrier, inc=1, device_id={"expert": peer}, device_id_type=MESH)

    for early, rs in FIRST_LOADS[1:]:
        for r in rs:
            w_load(r, early).start()
    for i in ROW_ORDER:
        for other in range(2):
            h_load(i, other).start()

    own_copies = [
        pltpu.make_async_copy(routes, all_routes.at[LAST], own_sem.at[0]),
        pltpu.make_async_copy(scores, all_scores.at[LAST], own_sem.at[1]),
        pltpu.make_async_copy(residual, rest, own_sem.at[2]),
    ]
    for copy in own_copies:
        copy.start()

    def route_copies(i):
        peer = {"expert": 2 * chip(-ahead(i)) + core}
        return [
            pltpu.make_async_remote_copy(
                src_ref=src, dst_ref=dst.at[i], send_sem=send.at[i], recv_sem=recv.at[i],
                device_id=peer, device_id_type=MESH,
            )
            for src, dst, send, recv in (
                (routes, all_routes, route_send, route_recv),
                (scores, all_scores, score_send, score_recv),
            )
        ]

    def ring_part(way, hop):
        first, second = HOPS[way][0], HOPS[way][2]
        return jnp.where(hop == 0, first, jnp.where(hop == 2, second, 2))

    def ring_copy(i, way, hop):
        k = 2 * i + way
        return pltpu.make_async_remote_copy(
            src_ref=part.at[k, ring_part(way, hop)],
            dst_ref=ring_in.at[hop, k],
            send_sem=ring_send.at[hop, k],
            recv_sem=ring_recv.at[hop, k],
            device_id={"tp": (up, down)[way]},
            device_id_type=MESH,
        )

    def late_copy(way, hop):
        return pltpu.make_async_remote_copy(
            src_ref=late.at[ring_part(way, hop), pl.ds(way * half, half)],
            dst_ref=late_in.at[hop, way],
            send_sem=late_send.at[hop, way],
            recv_sem=late_recv.at[hop, way],
            device_id={"tp": (up, down)[way]},
            device_id_type=MESH,
        )

    def hand_copy(i, early):
        first, count = (n_tp, n_early) if early else (0, n_tp)
        source, send, recv = (hand_a, ha_send, ha_recv) if early else (hand_b, hb_send, hb_recv)
        return pltpu.make_async_remote_copy(
            src_ref=source.at[i],
            dst_ref=blocks.at[i, pl.ds(first, count), 1],
            send_sem=send.at[i],
            recv_sem=recv.at[i],
            device_id={"expert": partner},
            device_id_type=MESH,
        )

    def goes_up(s):
        return s in (0, 1, n_tp)

    def raw_from(stage, s):
        return 0 if stage == 0 else 2 if goes_up(s) else 1

    def raw_copy(stage, s, other):
        i = raw_from(stage, s)
        source = (hand_b.at[i, s] if s < n_tp else hand_a.at[i, s - n_tp]) if other else blocks.at[i, s, 0]
        target = chip(1 if goes_up(s) == (stage == 0) else -1)
        return pltpu.make_async_remote_copy(
            src_ref=source,
            dst_ref=raw_in.at[stage, s, other],
            send_sem=raw_send.at[stage, s, other],
            recv_sem=raw_recv.at[stage, s, other],
            device_id={"expert": 2 * target + (1 - core if other else core)},
            device_id_type=MESH,
        )

    def raw_start(i, streams):
        for stage in range(2):
            chosen = [s for s in streams if raw_from(stage, s) == i]
            for s in chosen:
                for other in range(2):
                    raw_copy(stage, s, other).start()

    def raw_wait(stage, s):
        for other in range(2):
            pltpu.make_async_remote_copy(
                src_ref=raw_in.at[stage, s, other], dst_ref=raw_in.at[stage, s, other],
                send_sem=raw_send.at[stage, s, other], recv_sem=raw_recv.at[stage, s, other],
                device_id={"expert": partner}, device_id_type=MESH,
            ).wait_recv()

    def tok_copy(i, s, target):
        return pltpu.make_async_remote_copy(
            src_ref=tok.at[i - 1, s],
            dst_ref=tok_in.at[i - 1, s],
            send_sem=tok_send.at[i - 1, s],
            recv_sem=tok_recv.at[i - 1, s],
            device_id={"expert": 2 * target + core},
            device_id_type=MESH,
        )

    def left_rows(i):
        return h_buf[pl.ds(2 * i, 2)].reshape(2 * cap, h_buf.shape[2])

    def await_rows(i):
        for other in range(2):
            k = 2 * i + other
            pltpu.make_async_copy(hidden.at[0, 0], h_buf.at[k], h_sem.at[k]).wait()

    def product_early(i, r):
        product = jnp.dot(left_rows(i), w_early[r], preferred_element_type=f32)
        part[pl.ds(2 * i, 2), r] = product.astype(bf16).reshape(2, cap, TP_FIRST)

    def matmul_early(i, r):
        for new in (2, 3):
            @pl.when((i == 0) & (r == new))
            def _():
                w_load(new, True).wait()

        @pl.when(r == 0)
        def _():
            await_rows(i)

        product_early(i, r)
        for way in range(2):
            @pl.when(r == way)
            def _():
                ring_copy(i, way, 0).start()

    def product_late(i):
        product = jnp.dot(left_rows(i), w_late[...], preferred_element_type=f32).astype(bf16)
        for r in range(n_tp):
            piece = product[:, r * STREAM : (r + 1) * STREAM]
            blocks[i, r, 0] = piece[:cap]
            hand_b[i, r] = piece[cap:]

    def matmul_late(i, x):
        product_late(i)
        for begin in (1, 2):
            @pl.when(i == begin)
            def _():
                raw_start(begin, range(n_tp))

        hand_copy(i, False).start()

    def arrive(i, hop):
        for way in range(2):
            ring_copy(i, way, hop).wait_recv()
        for way in range(2):
            k, r = 2 * i + way, ring_part(way, hop + 1)
            part[k, r] = part[k, r] + ring_in[hop, k]
        for way in range(2):
            ring_copy(i, way, hop + 1).start()

    def arrive_last(i, x):
        hop = n_tp - 2
        for way in range(2):
            ring_copy(i, way, hop).wait_recv()
        for way in range(2):
            k = 2 * i + way
            for h in range(n_early):
                at = slice(h * STREAM, (h + 1) * STREAM)
                piece = part[k, n_tp - 1, :, at] + ring_in[hop, k, :, at]
                if way == 0:
                    blocks[i, n_tp + h, 0] = piece
                else:
                    hand_a[i, h] = piece

        for begin in range(3):
            @pl.when(i == begin)
            def _():
                raw_start(begin, range(n_tp, n_tp + n_early))

        @pl.when(i > 0)
        def _():
            hand_copy(i, True).start()

    def pick(j, rows):
        return jnp.dot(pick_hi[j], rows, preferred_element_type=f32) + jnp.dot(
            pick_lo[j], rows, preferred_element_type=f32
        )

    def weighted(i, s):
        return pick(i, blocks[i, s].reshape(2 * cap, STREAM))

    def chain(i, s):
        total = weighted(i, s)
        forward = (s < 2) | (s == n_tp)
        raw = (i == jnp.where(forward, 1, 2)) | (i == jnp.where(forward, 4, 3))

        @pl.when(raw)
        def _():
            stage = jnp.where(i > 2, 1, 0)
            raw_wait(stage, s)
            more = pick(jnp.where(i == 1, 0, i + LAST - 1), raw_in[stage, s].reshape(2 * cap, STREAM))
            tok[i - 1, s] = (total + more).astype(bf16)

        @pl.when(jnp.logical_not(raw))
        def _():
            tok_copy(i - 2, s, z).wait_recv()
            tok[i - 1, s] = (total + tok_in[i - 3, s].astype(f32)).astype(bf16)

        tok_copy(i, s, chip(jnp.where(lax.rem(i, 2) == 1, 1, -1))).start()

    def chain_first(i, s):
        @pl.when(s < n_tp)
        def _():
            hand_copy(i, False).wait_recv()

        @pl.when(s >= n_tp)
        def _():
            hand_copy(i, True).wait_recv()

        chain(i, s)

    def chain_end(s, total):
        for i in (LAST - 2, LAST - 1):
            tok_copy(i, s, z).wait_recv()
        return total + tok_in[LAST - 3, s].astype(f32) + tok_in[LAST - 2, s].astype(f32)

    def end_late(first, s):
        @pl.when(first == 1)
        def _():
            hand_copy(LAST, False).wait_recv()

        late[s] = chain_end(s, weighted(LAST, s)).astype(bf16)

    def late_step(i, x):
        @pl.when(x > 0)
        def _():
            for way in range(2):
                late_copy(way, x - 1).wait_recv()
            for way in range(2):
                here = pl.ds(way * half, half)
                r = ring_part(way, x)
                late[r, here] = late[r, here] + late_in[x - 1, way]

        for way in range(2):
            late_copy(way, x).start()

    def selection_table():
        rows = lax.broadcasted_iota(jnp.int32, (tokens, tokens), 0)
        cols = lax.broadcasted_iota(jnp.int32, (tokens, tokens), 1)
        earlier = jnp.where(rows < cols, 1.0, 0.0).astype(bf16)
        for j in range(1, LAST):
            for copy in route_copies(j):
                copy.wait_recv()
        for copy in own_copies[:2]:
            copy.wait()
        for j, (group, shift) in enumerate(SETS):
            chosen, value = all_routes[group], all_scores[group]
            share = value / jnp.sum(value, axis=0, keepdims=True)
            for q in range(2):
                same = chosen == 2 * chip(shift) + (1 - core if q else core)
                line = 2 * j + q
                counts[line : line + 1, :] = jnp.sum(jnp.where(same, 1.0, 0.0), axis=0, keepdims=True)
                table[96 + line : 97 + line, :] = jnp.sum(jnp.where(same, share, 0.0), axis=0, keepdims=True)
        used = 2 * len(SETS)
        counts[used:, :] = jnp.zeros((counts.shape[0] - used, tokens), f32)
        table[96 + used :, :] = jnp.zeros((32 - used, tokens), f32)
        member = counts[...]
        before = jnp.dot(member.astype(bf16), earlier, preferred_element_type=f32)
        second = lax.rem(lax.broadcasted_iota(jnp.int32, member.shape, 0), 2) == 1
        portion = table[96:128, :]
        portion_hi = portion.astype(bf16).astype(f32)
        table[0:32, :] = jnp.where(member > 0.5, before + jnp.where(second, float(cap), 0.0), -1.0)
        table[32:64, :] = portion_hi
        table[64:96, :] = portion - portion_hi
        upright[...] = jnp.transpose(table[...])

    def selection_sets(sets):
        column = lax.broadcasted_iota(jnp.int32, (tokens, 2 * cap), 1).astype(f32)
        for j in sets:
            own, other = (column == upright[:, 2 * j + q : 2 * j + q + 1] for q in range(2))
            for target, base in ((pick_hi, 32), (pick_lo, 64)):
                a, b = (upright[:, base + 2 * j + q : base + 2 * j + q + 1] for q in range(2))
                target[j] = jnp.where(own, a, jnp.where(other, b, 0.0)).astype(bf16)

    def selection(i, x):
        pl.when(x == 0)(selection_table)
        for stage, sets in enumerate(((0, 8, 1, 2), (3, 4, 9, 10), (5, 6, 7))):
            @pl.when(x == stage + 1)
            def _():
                selection_sets(sets)

    def nothing(i, x):
        pass

    kinds = (
        matmul_early, matmul_late, arrive, chain, end_late, late_step, selection, arrive_last, chain_first,
        nothing,
    )

    def first_late(r):
        w_load(r, False).wait()
        at = slice(r * STREAM, (r + 1) * STREAM)
        product = jnp.dot(left_rows(0), w_late[:, at], preferred_element_type=f32).astype(bf16)
        blocks[0, r, 0] = product[:cap]
        hand_b[0, r] = product[cap:]

    await_rows(0)
    first_late(0)
    pl.semaphore_wait(barrier, 2 + len(greeted))
    for i in range(1, LAST):
        for copy in route_copies(i):
            copy.start()
    raw_start(0, (0,))
    first_late(2)
    raw_start(0, (2,))
    for way in range(2):
        w_load(way, True).wait()
        product_early(0, way)
        ring_copy(0, way, 0).start()
    for r in (1, 3):
        first_late(r)
        raw_start(0, (r,))

    def steps(j, carry):
        word = jnp.int32(WORDS[0])
        for n in range(1, len(WORDS)):
            word = jnp.where(j == n, WORDS[n], word)

        def step(m, inner):
            code = lax.rem(lax.shift_right_logical(word, 10 * m), 1024)
            i, x = lax.rem(code // 8, 8), lax.rem(code, 8)

            def branch(kind):
                def run():
                    kind(i, x)

                return run

            lax.switch(code // 64, [branch(kind) for kind in kinds])
            return inner

        lax.fori_loop(0, 3, step, 0)
        return carry

    lax.fori_loop(0, len(WORDS), steps, 0)

    own_copies[2].wait()
    hand_copy(LAST, True).wait_recv()
    totals = []
    for h in range(n_early):
        at = slice(h * STREAM, (h + 1) * STREAM)
        totals.append(rest[:, at].astype(f32) + weighted(LAST, n_tp + h))
    for way in range(2):
        late_copy(way, n_tp - 2).wait_recv()
        here = slice(way * half, (way + 1) * half)
        mixed = late[n_tp - 1, here].astype(f32) + late_in[n_tp - 2, way].astype(f32)
        out[here, TP_FIRST:] = (rest[here, TP_FIRST:].astype(f32) + mixed).astype(bf16)
    for h in range(n_early):
        out[:, h * STREAM : (h + 1) * STREAM] = chain_end(n_tp + h, totals[h]).astype(bf16)

    def drain(i, carry):
        for hop in range(n_tp - 1):
            for way in range(2):
                ring_copy(i, way, hop).wait_send()

        @pl.when(i > 0)
        def _():
            for early in (False, True):
                hand_copy(i, early).wait_send()

        @pl.when((i > 0) & (i < LAST))
        def _():
            for s in range(blocks.shape[1]):
                @pl.when(i != (2 if goes_up(s) else 1))
                def _():
                    tok_copy(i, s, z).wait_send()

        return carry

    lax.fori_loop(0, CHIPS, drain, 0)
    for stage in range(2):
        for s in range(blocks.shape[1]):
            for other in range(2):
                raw_copy(stage, s, other).wait_send()
    for i in range(1, LAST):
        for copy in route_copies(i):
            copy.wait_send()
    for hop in range(n_tp - 1):
        for way in range(2):
            late_copy(way, hop).wait_send()


def on_device(hidden, down_weight, routes, route_weight, residual):
    sources, cap, units = hidden.shape[1:]
    tokens, width = residual.shape
    top = routes.shape[1]
    n_tp = len(SLICE_SHIFT)
    early = TP_FIRST // STREAM
    streams = n_tp + early
    bf16, f32 = jnp.bfloat16, jnp.float32
    any_space = pl.BlockSpec(memory_space=pl.ANY)
    dma = pltpu.SemaphoreType.DMA
    return pl.pallas_call(
        kernel,
        out_shape=pltpu.VMEM((tokens, width), bf16),
        in_specs=[any_space] * 5,
        out_specs=pl.BlockSpec(memory_space=pltpu.VMEM),
        scratch_shapes=[
            pltpu.VMEM((n_tp, units, TP_FIRST), bf16),
            pltpu.VMEM((units, n_tp * STREAM), bf16),
            pltpu.VMEM((sources, cap, units), bf16),
            pltpu.VMEM((sources, n_tp, cap, TP_FIRST), bf16),
            pltpu.VMEM((n_tp - 1, sources, cap, TP_FIRST), bf16),
            pltpu.VMEM((CHIPS, streams, 2, cap, STREAM), bf16),
            pltpu.VMEM((CHIPS, n_tp, cap, STREAM), bf16),
            pltpu.VMEM((CHIPS, early, cap, STREAM), bf16),
            pltpu.VMEM((2, streams, 2, cap, STREAM), bf16),
            pltpu.VMEM((LAST - 1, streams, tokens, STREAM), bf16),
            pltpu.VMEM((LAST - 1, streams, tokens, STREAM), bf16),
            pltpu.VMEM((n_tp, tokens, STREAM), bf16),
            pltpu.VMEM((n_tp - 1, 2, tokens // 2, STREAM), bf16),
            pltpu.VMEM((CHIPS, top, tokens), jnp.int32),
            pltpu.VMEM((CHIPS, top, tokens), f32),
            pltpu.VMEM((tokens, width), bf16),
            pltpu.VMEM((32, tokens), f32),
            pltpu.VMEM((128, tokens), f32),
            pltpu.VMEM((tokens, 128), f32),
            pltpu.VMEM((len(SETS), tokens, 2 * cap), bf16),
            pltpu.VMEM((len(SETS), tokens, 2 * cap), bf16),
            dma((n_tp,)),
            dma((n_tp,)),
            dma((sources,)),
            dma((3,)),
            dma((n_tp - 1, sources)),
            dma((n_tp - 1, sources)),
            dma((CHIPS,)),
            dma((CHIPS,)),
            dma((CHIPS,)),
            dma((CHIPS,)),
            dma((2, streams, 2)),
            dma((2, streams, 2)),
            dma((LAST - 1, streams)),
            dma((LAST - 1, streams)),
            dma((n_tp - 1, 2)),
            dma((n_tp - 1, 2)),
            dma((LAST,)),
            dma((LAST,)),
            dma((LAST,)),
            dma((LAST,)),
        ],
        compiler_params=pltpu.CompilerParams(
            collective_id=0, has_side_effects=True, vmem_limit_bytes=56 * 1024 * 1024
        ),
        name="moe_down_combine",
    )(hidden, down_weight, routes.T, route_weight.T, residual)


def solution(mesh):
    return jax.shard_map(
        on_device,
        mesh=mesh,
        in_specs=(
            P("expert", "dp", None, "tp"),
            P("expert", "tp", None),
            P(("dp", "expert"), None),
            P(("dp", "expert"), None),
            P(("dp", "expert"), "tp"),
        ),
        out_specs=P(("dp", "expert"), "tp"),
        check_vma=False,
    )
```
